512 devices in a mesh: doc: 16 (over y, x_hi), seq: 32 (over z, x_lo, core).
Axes of the slice: x: 4 (x_hi: 2, x_lo: 2; x = x_hi * 2 + x_lo), y: 8, z: 8, core: 2. Of those that a mesh axis runs over, the one named last changes fastest.
Arguments:
- enc_query: bfloat16 [16, 4096, 2048], P('doc', 'seq'), may hold values from -40 to 40
- enc_key: bfloat16 [16, 4096, 2048], P('doc', 'seq'), may hold values from -16 to 16
- enc_value: bfloat16 [16, 4096, 2048], P('doc', 'seq'), may hold values from -6 to 6
- sum_query: bfloat16 [16, 512, 2048], P('doc', 'seq'), may hold values from -70 to 70
- doc_len: int32 [16], P('doc'), may hold values from 1024 to 4096, as said below
- w_memory: bfloat16 [2, 2048, 2048], P(None, None, 'doc'), may hold values from -0.26367188 to 0.26367188
Outputs:
- encoder_out: bfloat16 [16, 4096, 2048], P('doc', 'seq')
- summary_out: bfloat16 [16, 512, 2048], P('doc', 'seq')
The draws below stay inside these ranges and needn't reach their ends.
Inputs may be any that keep to these rules, and one draw needn't show every extreme that they name: `doc_len`: at least one document has all 4096 tokens valid.
All inputs are finite; a program needn't handle non-finite values.
Results may differ from the reference program's by a relative error of at most 0.012.
Values may be sent and summed in bfloat16 or wider, within the bound.
A program may use at most 64 MiB of HBM per device.

```python
import jax
import jax.numpy as jnp
from jax import lax

HEADS = 32
HEAD_DIM = 64
D = 2048
SEQ_LEN = 4096
SUM_LEN = 512
DOCS = 16


def paired(key):
    base_key = jax.random.fold_in(key, 7)
    key_query, key_keys = jax.random.split(base_key)
    full_shape = (DOCS, SEQ_LEN, D)
    queries = 2.0 * jnp.clip(jax.random.normal(key_query, full_shape, jnp.float32), -6.0, 6.0)
    keys_out = 2.0 * jnp.clip(jax.random.normal(key_keys, full_shape, jnp.float32), -6.0, 6.0)
    return (queries, keys_out)


def draw_enc_query(key, part):
    return paired(key)[0].astype(jnp.bfloat16)


def draw_enc_key(key, part):
    return paired(key)[1].astype(jnp.bfloat16)


def draw_sum_query(key, part):
    base_key = jax.random.fold_in(key, 13)
    full_shape = (DOCS, SUM_LEN, D)
    values_out = 2.0 * jnp.clip(jax.random.normal(base_key, full_shape, jnp.float32), -6.0, 6.0)
    return values_out.astype(jnp.bfloat16)


def draw_doc_len(key, part):
    key_lengths, key_full = jax.random.split(jax.random.fold_in(key, 3))
    lengths = jax.random.randint(key_lengths, (DOCS,), SEQ_LEN // 4, SEQ_LEN + 1)
    full_doc = jax.random.randint(key_full, (), 0, DOCS)
    return jnp.where(jnp.arange(DOCS) == full_doc, SEQ_LEN, lengths).astype(jnp.int32)


def steps_of(stream_key, shape, cuts, least, high):
    def one(dim, parts):
        heights = jax.random.uniform(jax.random.fold_in(jax.random.fold_in(stream_key, 6), dim), (parts,), jnp.float32, least / len(cuts), high / len(cuts))
        return jnp.repeat(jnp.exp(heights), shape[dim] // parts).reshape((-1,) + (1,) * (len(shape) - dim - 1))

    level = one(*cuts[0])
    for cut in cuts[1:]:
        level = level * one(*cut)
    return level


def bell_draw(key, shape, scale, limit, shards=(), held_as=jnp.bfloat16):
    values = jax.random.normal(key, shape, jnp.float32) * scale
    if len(shards) > 0:
        values = steps_of(key, shape, shards, -0.22, 0.18) * values
    return jnp.clip(values, min=-limit, max=limit).astype(held_as)


def setup_inputs(seed: int = 0) -> dict:
    streams_of = jax.random.split(jax.random.key(seed), 7)
    return {
        "enc_query": draw_enc_query(jax.random.fold_in(streams_of[6], 71), 0),
        "enc_key": draw_enc_key(jax.random.fold_in(streams_of[6], 71), 0),
        "enc_value": bell_draw(streams_of[2], (DOCS, SEQ_LEN, D), 1.0, 6.0, ((0, 16), (1, 32))),
        "sum_query": draw_sum_query(jax.random.fold_in(streams_of[6], 71), 0),
        "doc_len": draw_doc_len(jax.random.fold_in(streams_of[6], 71), 0),
        "w_memory": bell_draw(streams_of[5], (2, D, D), (2.0 * D ** -0.5), 0.26367188, ((2, 16),)),
    }


def attend(queries, keys_in, values_in, length):
    scores = jnp.dot(queries, keys_in.T, preferred_element_type=jnp.float32) * (HEAD_DIM ** -0.5)
    key_valid = jnp.arange(keys_in.shape[0]) < length
    scores = jnp.where(key_valid[None, :], scores, -1e30)
    row_max = jnp.max(scores, axis=-1, keepdims=True)
    weights = jnp.exp(scores - row_max)
    denominator = jnp.sum(weights, axis=-1, keepdims=True)
    weighted = jnp.dot(weights.astype(jnp.bfloat16), values_in, preferred_element_type=jnp.float32)
    return (weighted / denominator).astype(jnp.bfloat16)


def split_heads(matrix, row_count):
    return matrix.reshape(row_count, HEADS, HEAD_DIM).transpose(1, 0, 2)


def reference(enc_query, enc_key, enc_value, sum_query, doc_len, w_memory):
    def one_doc(doc_items):
        queries, keys_in, values_in, summary, length = doc_items
        context = lax.map(lambda triple: attend(triple[0], triple[1], triple[2], length),
                          (split_heads(queries, SEQ_LEN), split_heads(keys_in, SEQ_LEN), split_heads(values_in, SEQ_LEN)))
        encoder_doc = context.transpose(1, 0, 2).reshape(SEQ_LEN, D)
        mem_keys = jnp.dot(encoder_doc, w_memory[0], preferred_element_type=jnp.float32).astype(jnp.bfloat16)
        mem_values = jnp.dot(encoder_doc, w_memory[1], preferred_element_type=jnp.float32).astype(jnp.bfloat16)
        answer = lax.map(lambda triple: attend(triple[0], triple[1], triple[2], length),
                         (split_heads(summary, SUM_LEN), split_heads(mem_keys, SEQ_LEN), split_heads(mem_values, SEQ_LEN)))
        return encoder_doc, answer.transpose(1, 0, 2).reshape(SUM_LEN, D)

    encoder_out, summary_out = lax.map(one_doc, (enc_query, enc_key, enc_value, sum_query, doc_len))
    return encoder_out, summary_out
```

```python
import math

import jax
import jax.numpy as jnp
from jax import lax
from jax.sharding import PartitionSpec as P

HEAD_DIM = 64


def attend_heads(queries, keys_all, values_all, length, head_dim):
    row_count = queries.shape[0]
    feature_width = queries.shape[1]
    head_count = feature_width // head_dim
    block_rows = math.gcd(row_count, 512)
    grouped = queries.reshape(row_count // block_rows, block_rows, head_count, head_dim)
    key_heads = keys_all.reshape(-1, head_count, head_dim)
    value_heads = values_all.reshape(-1, head_count, head_dim)
    key_valid = jnp.arange(key_heads.shape[0]) < length

    def one_block(query_block):
        scores = jnp.einsum(
            "qhd,khd->hqk", query_block, key_heads, preferred_element_type=jnp.float32
        ) * head_dim ** (-0.5)
        scores = jnp.where(key_valid[None, None, :], scores, -1e30)
        row_max = jnp.max(scores, axis=-1, keepdims=True)
        weights = jnp.exp(scores - row_max)
        denominator = jnp.sum(weights, axis=-1)
        weighted = jnp.einsum(
            "hqk,khd->qhd",
            weights.astype(jnp.bfloat16),
            value_heads,
            preferred_element_type=jnp.float32,
        )
        return (weighted / denominator.T[:, :, None]).astype(jnp.bfloat16)

    return lax.map(one_block, grouped).reshape(row_count, feature_width)


def shards(enc_query, enc_key, enc_value, sum_query, doc_len, w_memory):
    head_dim = HEAD_DIM
    length = doc_len[0]
    n_seq = lax.axis_size("seq")
    core = lax.axis_index("seq") % 2
    half = w_memory.shape[1] // 2
    w_mine = lax.dynamic_slice_in_dim(w_memory, core * half, half, axis=1)
    w_mine = lax.all_gather(w_mine, "doc", axis=2, tiled=True)
    w_other = lax.ppermute(w_mine, "seq", perm=[(i, i ^ 1) for i in range(n_seq)])

    head_query, head_key, head_value = (
        lax.all_to_all(enc_query[0], "seq", split_axis=1, concat_axis=0, tiled=True),
        lax.all_to_all(enc_key[0], "seq", split_axis=1, concat_axis=0, tiled=True),
        lax.all_to_all(enc_value[0], "seq", split_axis=1, concat_axis=0, tiled=True),
    )
    summary_heads = lax.all_to_all(sum_query[0], "seq", split_axis=1, concat_axis=0, tiled=True)
    context = attend_heads(head_query, head_key, head_value, length, head_dim)
    encoder_out = lax.all_to_all(context, "seq", split_axis=0, concat_axis=1, tiled=True)

    enc_mine = lax.dynamic_slice_in_dim(encoder_out, core * half, half, axis=1)
    enc_other = lax.dynamic_slice_in_dim(encoder_out, (1 - core) * half, half, axis=1)
    made = jnp.einsum("tf,kfc->tkc", enc_mine, w_mine, preferred_element_type=jnp.float32)
    made = made + jnp.einsum("tf,kfc->tkc", enc_other, w_other, preferred_element_type=jnp.float32)
    memory_rows = made.astype(jnp.bfloat16)
    memory_local = lax.all_to_all(memory_rows, "seq", split_axis=2, concat_axis=0, tiled=True)
    memory_keys = memory_local[:, 0, :]
    memory_values = memory_local[:, 1, :]
    answer = attend_heads(summary_heads, memory_keys, memory_values, length, head_dim)
    summary_out = lax.all_to_all(answer, "seq", split_axis=0, concat_axis=1, tiled=True)
    return (encoder_out[None], summary_out[None])


def solution(mesh):
    in_specs = (
        P("doc", "seq", None),
        P("doc", "seq", None),
        P("doc", "seq", None),
        P("doc", "seq", None),
        P("doc"),
        P(None, None, "doc"),
    )
    out_specs = (P("doc", "seq", None), P("doc", "seq", None))
    return jax.shard_map(shards, mesh=mesh, in_specs=in_specs, out_specs=out_specs, check_vma=False)
```

```python
import jax
import jax.numpy as jnp
from jax import lax
from jax.experimental import pallas as pl
from jax.experimental.pallas import tpu as pltpu
from jax.sharding import PartitionSpec as P

HEAD_DIM = 64


def _attend_kernel(len_ref, q_ref, k_ref, v_ref, o_ref):
    scores = lax.dot_general(
        q_ref[...], k_ref[...], (((1,), (1,)), ((), ())), preferred_element_type=jnp.float32
    ) * HEAD_DIM ** (-0.5)
    key_pos = lax.broadcasted_iota(jnp.int32, scores.shape, 1)
    scores = jnp.where(key_pos < len_ref[0], scores, -1e30)
    row_max = jnp.max(scores, axis=1, keepdims=True)
    weights = jnp.exp(scores - row_max)
    denominator = jnp.sum(weights, axis=1, keepdims=True)
    weighted = jnp.dot(weights.astype(jnp.bfloat16), v_ref[...], preferred_element_type=jnp.float32)
    o_ref[...] = (weighted / denominator).astype(o_ref.dtype)


def attend_head(queries, keys_in, values_in, length, block_rows=256):
    nq, width = queries.shape
    nk = keys_in.shape[0]
    block_rows = min(block_rows, nq)
    grid_spec = pltpu.PrefetchScalarGridSpec(
        num_scalar_prefetch=1,
        grid=(nq // block_rows,),
        in_specs=[
            pl.BlockSpec((block_rows, width), lambda i, n: (i, 0)),
            pl.BlockSpec((nk, width), lambda i, n: (0, 0)),
            pl.BlockSpec((nk, width), lambda i, n: (0, 0)),
        ],
        out_specs=pl.BlockSpec((block_rows, width), lambda i, n: (i, 0)),
    )
    cost = pl.CostEstimate(
        flops=4 * nq * nk * width,
        transcendentals=nq * nk,
        bytes_accessed=2 * (2 * nq * width + 2 * nk * width),
    )
    return pl.pallas_call(
        _attend_kernel,
        grid_spec=grid_spec,
        out_shape=jax.ShapeDtypeStruct((nq, width), jnp.bfloat16),
        cost_estimate=cost,
        compiler_params=pltpu.CompilerParams(vmem_limit_bytes=48 * 1024 * 1024),
    )(length.reshape(1), queries, keys_in, values_in)


def shards(enc_query, enc_key, enc_value, sum_query, doc_len, w_memory):
    length = doc_len[0]
    n_seq = lax.axis_size("seq")
    core = lax.axis_index("seq") % 2
    sibling = [(i, i ^ 1) for i in range(n_seq)]
    half = w_memory.shape[2] // 2
    w_half = lax.dynamic_slice_in_dim(w_memory, core * half, half, axis=2)
    w_half = lax.all_gather(w_half, "doc", axis=2, tiled=True)

    head_query, head_key, head_value = (
        lax.all_to_all(enc_query[0], "seq", split_axis=1, concat_axis=0, tiled=True),
        lax.all_to_all(enc_key[0], "seq", split_axis=1, concat_axis=0, tiled=True),
        lax.all_to_all(enc_value[0], "seq", split_axis=1, concat_axis=0, tiled=True),
    )
    summary_heads = lax.all_to_all(sum_query[0], "seq", split_axis=1, concat_axis=0, tiled=True)
    context = attend_head(head_query, head_key, head_value, length)
    encoder_out = lax.all_to_all(context, "seq", split_axis=0, concat_axis=1, tiled=True)

    enc_pair = jnp.concatenate([encoder_out, lax.ppermute(encoder_out, "seq", sibling)], axis=0)
    made = jnp.einsum("tf,kfc->tkc", enc_pair, w_half, preferred_element_type=jnp.float32)
    made = made.astype(jnp.bfloat16).reshape(2, encoder_out.shape[0], 2, -1, 1, half)
    own, received = made[0], lax.ppermute(made[1], "seq", sibling)
    memory_rows = jnp.where(core == 0, jnp.concatenate([own, received], axis=3),
                            jnp.concatenate([received, own], axis=3))
    memory_rows = memory_rows.reshape(encoder_out.shape[0], 2, -1)
    memory_local = lax.all_to_all(memory_rows, "seq", split_axis=2, concat_axis=0, tiled=True)
    memory_keys = memory_local[:, 0, :]
    memory_values = memory_local[:, 1, :]
    answer = attend_head(summary_heads, memory_keys, memory_values, length)
    summary_out = lax.all_to_all(answer, "seq", split_axis=0, concat_axis=1, tiled=True)
    return (encoder_out[None], summary_out[None])


def solution(mesh):
    in_specs = (
        P("doc", "seq", None),
        P("doc", "seq", None),
        P("doc", "seq", None),
        P("doc", "seq", None),
        P("doc"),
        P(None, None, "doc"),
    )
    out_specs = (P("doc", "seq", None), P("doc", "seq", None))
    return jax.shard_map(shards, mesh=mesh, in_specs=in_specs, out_specs=out_specs, check_vma=False)
```

```python
import jax
import jax.numpy as jnp
from jax import lax
from jax.experimental import pallas as pl
from jax.experimental.pallas import tpu as pltpu
from jax.sharding import PartitionSpec as P

HEAD_DIM = 64


def _attend_kernel(len_ref, q_ref, k_ref, v_ref, o_ref):
    scores = lax.dot_general(
        q_ref[...], k_ref[...], (((1,), (1,)), ((), ())), preferred_element_type=jnp.float32
    ) * HEAD_DIM ** (-0.5)
    key_pos = lax.broadcasted_iota(jnp.int32, scores.shape, 1)
    scores = jnp.where(key_pos < len_ref[0], scores, -1e30)
    row_max = jnp.max(scores, axis=1, keepdims=True)
    weights = jnp.exp(scores - row_max)
    denominator = jnp.sum(weights, axis=1, keepdims=True)
    weighted = jnp.dot(weights.astype(jnp.bfloat16), v_ref[...], preferred_element_type=jnp.float32)
    o_ref[...] = (weighted / denominator).astype(o_ref.dtype)


def attend_head(queries, keys_in, values_in, length, block_rows=256):
    nq, width = queries.shape
    nk = keys_in.shape[0]
    block_rows = min(block_rows, nq)
    grid_spec = pltpu.PrefetchScalarGridSpec(
        num_scalar_prefetch=1,
        grid=(nq // block_rows,),
        in_specs=[
            pl.BlockSpec((block_rows, width), lambda i, n: (i, 0)),
            pl.BlockSpec((nk, width), lambda i, n: (0, 0)),
            pl.BlockSpec((nk, width), lambda i, n: (0, 0)),
        ],
        out_specs=pl.BlockSpec((block_rows, width), lambda i, n: (i, 0)),
    )
    cost = pl.CostEstimate(
        flops=4 * nq * nk * width,
        transcendentals=nq * nk,
        bytes_accessed=2 * (2 * nq * width + 2 * nk * width),
    )
    return pl.pallas_call(
        _attend_kernel,
        grid_spec=grid_spec,
        out_shape=jax.ShapeDtypeStruct((nq, width), jnp.bfloat16),
        cost_estimate=cost,
        compiler_params=pltpu.CompilerParams(vmem_limit_bytes=48 * 1024 * 1024),
    )(length.reshape(1), queries, keys_in, values_in)


def shards(enc_query, enc_key, enc_value, sum_query, doc_len, w_memory):
    length = doc_len[0]
    n_seq = lax.axis_size("seq")
    core = lax.axis_index("seq") % 2
    sibling = [(i, i ^ 1) for i in range(n_seq)]
    half = w_memory.shape[2] // 2
    w_halves = [
        lax.all_gather(lax.dynamic_slice_in_dim(w_memory[m], core * half, half, axis=1), "doc", axis=1, tiled=True)
        for m in range(2)
    ]

    head_query, head_key, head_value = (
        lax.all_to_all(enc_query[0], "seq", split_axis=1, concat_axis=0, tiled=True),
        lax.all_to_all(enc_key[0], "seq", split_axis=1, concat_axis=0, tiled=True),
        lax.all_to_all(enc_value[0], "seq", split_axis=1, concat_axis=0, tiled=True),
    )
    summary_heads = lax.all_to_all(sum_query[0], "seq", split_axis=1, concat_axis=0, tiled=True)
    context = attend_head(head_query, head_key, head_value, length)
    encoder_out = lax.all_to_all(context, "seq", split_axis=0, concat_axis=1, tiled=True)

    rows = encoder_out.shape[0]
    enc_pair = jnp.concatenate([encoder_out, lax.ppermute(encoder_out, "seq", sibling)], axis=0)
    memory = []
    for w_half in w_halves:
        made = jnp.dot(enc_pair, w_half, preferred_element_type=jnp.float32).astype(jnp.bfloat16)
        made = made.reshape(2, rows, -1, half).transpose(0, 2, 1, 3)
        own, received = made[0], lax.ppermute(made[1], "seq", sibling)
        by_head = jnp.where(core == 0, jnp.stack([own, received], axis=1), jnp.stack([received, own], axis=1))
        by_head = by_head.reshape(n_seq, rows, half)
        memory.append(lax.all_to_all(by_head, "seq", split_axis=0, concat_axis=0, tiled=True).reshape(-1, half))
    memory_keys, memory_values = memory
    answer = attend_head(summary_heads, memory_keys, memory_values, length)
    summary_out = lax.all_to_all(answer, "seq", split_axis=0, concat_axis=1, tiled=True)
    return (encoder_out[None], summary_out[None])


def solution(mesh):
    in_specs = (
        P("doc", "seq", None),
        P("doc", "seq", None),
        P("doc", "seq", None),
        P("doc", "seq", None),
        P("doc"),
        P(None, None, "doc"),
    )
    out_specs = (P("doc", "seq", None), P("doc", "seq", None))
    return jax.shard_map(shards, mesh=mesh, in_specs=in_specs, out_specs=out_specs, check_vma=False)
```

```python
import jax
import jax.numpy as jnp
from jax import lax
from jax.experimental import pallas as pl
from jax.experimental.pallas import tpu as pltpu
from jax.sharding import PartitionSpec as P

HEAD_DIM = 64


def _attend_kernel(len_ref, q_ref, k_ref, v_ref, o_ref):
    scores = lax.dot_general(
        q_ref[...], k_ref[...], (((1,), (1,)), ((), ())), preferred_element_type=jnp.float32
    ) * HEAD_DIM ** (-0.5)
    key_pos = lax.broadcasted_iota(jnp.int32, scores.shape, 1)
    scores = jnp.where(key_pos < len_ref[0], scores, -1e30)
    row_max = jnp.max(scores, axis=1, keepdims=True)
    weights = jnp.exp(scores - row_max)
    denominator = jnp.sum(weights, axis=1, keepdims=True)
    weighted = jnp.dot(weights.astype(jnp.bfloat16), v_ref[...], preferred_element_type=jnp.float32)
    o_ref[...] = (weighted / denominator).astype(o_ref.dtype)


def attend_head(queries, keys_in, values_in, length, block_rows=256):
    nq, width = queries.shape
    nk = keys_in.shape[0]
    block_rows = min(block_rows, nq)
    grid_spec = pltpu.PrefetchScalarGridSpec(
        num_scalar_prefetch=1,
        grid=(nq // block_rows,),
        in_specs=[
            pl.BlockSpec((block_rows, width), lambda i, n: (i, 0)),
            pl.BlockSpec((nk, width), lambda i, n: (0, 0)),
            pl.BlockSpec((nk, width), lambda i, n: (0, 0)),
        ],
        out_specs=pl.BlockSpec((block_rows, width), lambda i, n: (i, 0)),
    )
    cost = pl.CostEstimate(
        flops=4 * nq * nk * width,
        transcendentals=nq * nk,
        bytes_accessed=2 * (2 * nq * width + 2 * nk * width),
    )
    return pl.pallas_call(
        _attend_kernel,
        grid_spec=grid_spec,
        out_shape=jax.ShapeDtypeStruct((nq, width), jnp.bfloat16),
        cost_estimate=cost,
        compiler_params=pltpu.CompilerParams(vmem_limit_bytes=48 * 1024 * 1024),
    )(length.reshape(1), queries, keys_in, values_in)


def shards(enc_query, enc_key, enc_value, sum_query, doc_len, w_memory):
    length = doc_len[0]
    n_seq = lax.axis_size("seq")
    core = lax.axis_index("seq") % 2
    sibling = [(i, i ^ 1) for i in range(n_seq)]
    half = w_memory.shape[2] // 2
    w_half = lax.all_gather(lax.dynamic_slice_in_dim(w_memory, core * half, half, axis=2), "doc", axis=2, tiled=True)

    rows, sum_rows = enc_query.shape[1], sum_query.shape[1]
    both_query = lax.all_to_all(
        jnp.concatenate([enc_query[0], sum_query[0]], axis=0), "seq", split_axis=1, concat_axis=0, tiled=True
    ).reshape(n_seq, rows + sum_rows, -1)
    head_query = both_query[:, :rows].reshape(n_seq * rows, -1)
    summary_heads = both_query[:, rows:].reshape(n_seq * sum_rows, -1)
    head_key = lax.all_to_all(enc_key[0], "seq", split_axis=1, concat_axis=0, tiled=True)
    head_value = lax.all_to_all(enc_value[0], "seq", split_axis=1, concat_axis=0, tiled=True)
    context = attend_head(head_query, head_key, head_value, length)
    encoder_out = lax.all_to_all(context, "seq", split_axis=0, concat_axis=1, tiled=True)

    enc_pair = jnp.concatenate([encoder_out, lax.ppermute(encoder_out, "seq", sibling)], axis=0)
    made = jnp.einsum("tf,kfc->ktc", enc_pair, w_half, preferred_element_type=jnp.float32).astype(jnp.bfloat16)
    made = made.reshape(2, 2, rows, -1, half).transpose(1, 3, 0, 2, 4)
    own, received = made[0], lax.ppermute(made[1], "seq", sibling)
    by_head = jnp.where(core == 0, jnp.stack([own, received], axis=1), jnp.stack([received, own], axis=1))
    by_head = by_head.reshape(n_seq, 2, rows, half)
    memory = lax.all_to_all(by_head, "seq", split_axis=0, concat_axis=2, tiled=True)
    memory_keys, memory_values = memory[0, 0], memory[0, 1]
    answer = attend_head(summary_heads, memory_keys, memory_values, length)
    summary_out = lax.all_to_all(answer, "seq", split_axis=0, concat_axis=1, tiled=True)
    return (encoder_out[None], summary_out[None])


def solution(mesh):
    in_specs = (
        P("doc", "seq", None),
        P("doc", "seq", None),
        P("doc", "seq", None),
        P("doc", "seq", None),
        P("doc"),
        P(None, None, "doc"),
    )
    out_specs = (P("doc", "seq", None), P("doc", "seq", None))
    return jax.shard_map(shards, mesh=mesh, in_specs=in_specs, out_specs=out_specs, check_vma=False)
```

```python
import jax
import jax.numpy as jnp
from jax import lax
from jax.experimental import pallas as pl
from jax.experimental.pallas import tpu as pltpu
from jax.sharding import PartitionSpec as P

HEAD_DIM = 64


def _attend_kernel(len_ref, q_ref, k_ref, v_ref, o_ref):
    scores = lax.dot_general(
        q_ref[...], k_ref[...], (((1,), (1,)), ((), ())), preferred_element_type=jnp.float32
    ) * HEAD_DIM ** (-0.5)
    key_pos = lax.broadcasted_iota(jnp.int32, scores.shape, 1)
    scores = jnp.where(key_pos < len_ref[0], scores, -1e30)
    row_max = jnp.max(scores, axis=1, keepdims=True)
    weights = jnp.exp(scores - row_max)
    denominator = jnp.sum(weights, axis=1, keepdims=True)
    weighted = jnp.dot(weights.astype(jnp.bfloat16), v_ref[...], preferred_element_type=jnp.float32)
    o_ref[...] = (weighted / denominator).astype(o_ref.dtype)


def attend_head(queries, keys_in, values_in, length, block_rows=256):
    nq, width = queries.shape
    nk = keys_in.shape[0]
    block_rows = min(block_rows, nq)
    grid_spec = pltpu.PrefetchScalarGridSpec(
        num_scalar_prefetch=1,
        grid=(nq // block_rows,),
        in_specs=[
            pl.BlockSpec((block_rows, width), lambda i, n: (i, 0)),
            pl.BlockSpec((nk, width), lambda i, n: (0, 0)),
            pl.BlockSpec((nk, width), lambda i, n: (0, 0)),
        ],
        out_specs=pl.BlockSpec((block_rows, width), lambda i, n: (i, 0)),
    )
    cost = pl.CostEstimate(
        flops=4 * nq * nk * width,
        transcendentals=nq * nk,
        bytes_accessed=2 * (2 * nq * width + 2 * nk * width),
    )
    return pl.pallas_call(
        _attend_kernel,
        grid_spec=grid_spec,
        out_shape=jax.ShapeDtypeStruct((nq, width), jnp.bfloat16),
        cost_estimate=cost,
        compiler_params=pltpu.CompilerParams(vmem_limit_bytes=48 * 1024 * 1024),
    )(length.reshape(1), queries, keys_in, values_in)


def shards(enc_query, enc_key, enc_value, sum_query, doc_len, w_memory):
    length = doc_len[0]
    n_seq = lax.axis_size("seq")
    core = lax.axis_index("seq") % 2
    sibling = [(i, i ^ 1) for i in range(n_seq)]
    half = w_memory.shape[2] // 2
    w_half = lax.dynamic_slice_in_dim(w_memory, core * half, half, axis=2)
    w_half = lax.all_gather(w_half, "doc_x", axis=2, tiled=True)
    w_half = lax.all_gather(w_half, "doc_y", axis=2, tiled=True)

    rows, sum_rows = enc_query.shape[1], sum_query.shape[1]
    mixed = lax.all_to_all(
        jnp.concatenate([enc_query[0], enc_key[0], enc_value[0], sum_query[0]], axis=0),
        "seq", split_axis=1, concat_axis=0, tiled=True,
    ).reshape(n_seq, 3 * rows + sum_rows, -1)
    head_query, head_key, head_value = (mixed[:, i * rows:(i + 1) * rows].reshape(n_seq * rows, -1) for i in range(3))
    summary_heads = mixed[:, 3 * rows:].reshape(n_seq * sum_rows, -1)
    context = attend_head(head_query, head_key, head_value, length)
    encoder_out = lax.all_to_all(context, "seq", split_axis=0, concat_axis=1, tiled=True)

    enc_pair = jnp.concatenate([encoder_out, lax.ppermute(encoder_out, "seq", sibling)], axis=0)
    made = jnp.einsum("tf,kfc->ktc", enc_pair, w_half, preferred_element_type=jnp.float32).astype(jnp.bfloat16)
    made = made.reshape(2, 2, rows, -1, half).transpose(1, 3, 0, 2, 4)
    own, received = made[0], lax.ppermute(made[1], "seq", sibling)
    by_head = jnp.where(core == 0, jnp.stack([own, received], axis=1), jnp.stack([received, own], axis=1))
    by_head = by_head.reshape(n_seq, 2, rows, half)
    memory = lax.all_to_all(by_head, "seq", split_axis=0, concat_axis=2, tiled=True)
    memory_keys, memory_values = memory[0, 0], memory[0, 1]
    answer = attend_head(summary_heads, memory_keys, memory_values, length)
    summary_out = lax.all_to_all(answer, "seq", split_axis=0, concat_axis=1, tiled=True)
    return (encoder_out[None], summary_out[None])


def solution(mesh):
    n_doc = mesh.shape["doc"]
    split = jax.sharding.Mesh(mesh.devices.reshape(n_doc // 2, 2, mesh.shape["seq"]), ("doc_y", "doc_x", "seq"))
    doc = ("doc_y", "doc_x")
    in_specs = (
        P(doc, "seq", None),
        P(doc, "seq", None),
        P(doc, "seq", None),
        P(doc, "seq", None),
        P(doc),
        P(None, None, doc),
    )
    out_specs = (P(doc, "seq", None), P(doc, "seq", None))
    return jax.shard_map(shards, mesh=split, in_specs=in_specs, out_specs=out_specs, check_vma=False)
```

```python
import jax
import jax.numpy as jnp
from jax import lax
from jax.experimental import pallas as pl
from jax.experimental.pallas import tpu as pltpu
from jax.sharding import PartitionSpec as P

HEAD_DIM = 64


def _attend_kernel(len_ref, q_ref, k_ref, v_ref, o_ref):
    scores = lax.dot_general(
        q_ref[...], k_ref[...], (((1,), (1,)), ((), ())), preferred_element_type=jnp.float32
    ) * HEAD_DIM ** (-0.5)
    key_pos = lax.broadcasted_iota(jnp.int32, scores.shape, 1)
    scores = jnp.where(key_pos < len_ref[0], scores, -1e30)
    row_max = jnp.max(scores, axis=1, keepdims=True)
    weights = jnp.exp(scores - row_max)
    denominator = jnp.sum(weights, axis=1, keepdims=True)
    weighted = jnp.dot(weights.astype(jnp.bfloat16), v_ref[...], preferred_element_type=jnp.float32)
    o_ref[...] = (weighted / denominator).astype(o_ref.dtype)


def attend_head(queries, keys_in, values_in, length, block_rows=256):
    nq, width = queries.shape
    nk = keys_in.shape[0]
    block_rows = min(block_rows, nq)
    grid_spec = pltpu.PrefetchScalarGridSpec(
        num_scalar_prefetch=1,
        grid=(nq // block_rows,),
        in_specs=[
            pl.BlockSpec((block_rows, width), lambda i, n: (i, 0)),
            pl.BlockSpec((nk, width), lambda i, n: (0, 0)),
            pl.BlockSpec((nk, width), lambda i, n: (0, 0)),
        ],
        out_specs=pl.BlockSpec((block_rows, width), lambda i, n: (i, 0)),
    )
    cost = pl.CostEstimate(
        flops=4 * nq * nk * width,
        transcendentals=nq * nk,
        bytes_accessed=2 * (2 * nq * width + 2 * nk * width),
    )
    return pl.pallas_call(
        _attend_kernel,
        grid_spec=grid_spec,
        out_shape=jax.ShapeDtypeStruct((nq, width), jnp.bfloat16),
        cost_estimate=cost,
        compiler_params=pltpu.CompilerParams(vmem_limit_bytes=48 * 1024 * 1024),
    )(length.reshape(1), queries, keys_in, values_in)


def shards(enc_query, enc_key, enc_value, sum_query, doc_len, w_memory):
    length = doc_len[0]
    n_seq = lax.axis_size("seq")
    core = lax.axis_index("seq") % 2
    sibling = [(i, i ^ 1) for i in range(n_seq)]
    half = w_memory.shape[2] // 2
    w_half = lax.dynamic_slice_in_dim(w_memory, core * half, half, axis=2)
    w_pair = lax.ppermute(w_half, "doc_x", perm=[(0, 1), (1, 0)])
    w_half = jnp.where(lax.axis_index("doc_x") == 0, jnp.concatenate([w_half, w_pair], axis=2),
                       jnp.concatenate([w_pair, w_half], axis=2))
    w_half = lax.all_gather(w_half, "doc_y", axis=2, tiled=True)

    rows, sum_rows = enc_query.shape[1], sum_query.shape[1]
    mixed = lax.all_to_all(
        jnp.concatenate([enc_query[0], enc_key[0], enc_value[0], sum_query[0]], axis=0),
        "seq", split_axis=1, concat_axis=0, tiled=True,
    ).reshape(n_seq, 3 * rows + sum_rows, -1)
    head_query, head_key, head_value = (mixed[:, i * rows:(i + 1) * rows].reshape(n_seq * rows, -1) for i in range(3))
    summary_heads = mixed[:, 3 * rows:].reshape(n_seq * sum_rows, -1)
    context = attend_head(head_query, head_key, head_value, length)
    encoder_out = lax.all_to_all(context, "seq", split_axis=0, concat_axis=1, tiled=True)

    enc_pair = jnp.concatenate([encoder_out, lax.ppermute(encoder_out, "seq", sibling)], axis=0)
    made = jnp.einsum("tf,kfc->ktc", enc_pair, w_half, preferred_element_type=jnp.float32).astype(jnp.bfloat16)
    made = made.reshape(2, 2, rows, -1, half).transpose(1, 3, 0, 2, 4)
    own, received = made[0], lax.ppermute(made[1], "seq", sibling)
    by_head = jnp.where(core == 0, jnp.stack([own, received], axis=1), jnp.stack([received, own], axis=1))
    by_head = by_head.reshape(n_seq, 2, rows, half)
    memory = lax.all_to_all(by_head, "seq", split_axis=0, concat_axis=2, tiled=True)
    memory_keys, memory_values = memory[0, 0], memory[0, 1]
    answer = attend_head(summary_heads, memory_keys, memory_values, length)
    summary_out = lax.all_to_all(answer, "seq", split_axis=0, concat_axis=1, tiled=True)
    return (encoder_out[None], summary_out[None])


def solution(mesh):
    n_doc = mesh.shape["doc"]
    split = jax.sharding.Mesh(mesh.devices.reshape(n_doc // 2, 2, mesh.shape["seq"]), ("doc_y", "doc_x", "seq"))
    doc = ("doc_y", "doc_x")
    in_specs = (
        P(doc, "seq", None),
        P(doc, "seq", None),
        P(doc, "seq", None),
        P(doc, "seq", None),
        P(doc),
        P(None, None, doc),
    )
    out_specs = (P(doc, "seq", None), P(doc, "seq", None))
    return jax.shard_map(shards, mesh=split, in_specs=in_specs, out_specs=out_specs, check_vma=False)
```

```python
import jax
import jax.numpy as jnp
from jax import lax
from jax.experimental import pallas as pl
from jax.experimental.pallas import tpu as pltpu
from jax.sharding import PartitionSpec as P

HEAD_DIM = 64


def _attend_kernel(len_ref, q_ref, k_ref, v_ref, o_ref):
    scores = lax.dot_general(
        q_ref[...], k_ref[...], (((1,), (1,)), ((), ())), preferred_element_type=jnp.float32
    ) * HEAD_DIM ** (-0.5)
    key_pos = lax.broadcasted_iota(jnp.int32, scores.shape, 1)
    scores = jnp.where(key_pos < len_ref[0], scores, -1e30)
    row_max = jnp.max(scores, axis=1, keepdims=True)
    weights = jnp.exp(scores - row_max)
    denominator = jnp.sum(weights, axis=1, keepdims=True)
    weighted = jnp.dot(weights.astype(jnp.bfloat16), v_ref[...], preferred_element_type=jnp.float32)
    o_ref[...] = (weighted / denominator).astype(o_ref.dtype)


def attend_head(queries, keys_in, values_in, length, block_rows=256):
    nq, width = queries.shape
    nk = keys_in.shape[0]
    block_rows = min(block_rows, nq)
    grid_spec = pltpu.PrefetchScalarGridSpec(
        num_scalar_prefetch=1,
        grid=(nq // block_rows,),
        in_specs=[
            pl.BlockSpec((block_rows, width), lambda i, n: (i, 0)),
            pl.BlockSpec((nk, width), lambda i, n: (0, 0)),
            pl.BlockSpec((nk, width), lambda i, n: (0, 0)),
        ],
        out_specs=pl.BlockSpec((block_rows, width), lambda i, n: (i, 0)),
    )
    cost = pl.CostEstimate(
        flops=4 * nq * nk * width,
        transcendentals=nq * nk,
        bytes_accessed=2 * (2 * nq * width + 2 * nk * width),
    )
    return pl.pallas_call(
        _attend_kernel,
        grid_spec=grid_spec,
        out_shape=jax.ShapeDtypeStruct((nq, width), jnp.bfloat16),
        cost_estimate=cost,
        compiler_params=pltpu.CompilerParams(vmem_limit_bytes=48 * 1024 * 1024),
    )(length.reshape(1), queries, keys_in, values_in)


MESH = pl.DeviceIdType.MESH


def _attend_scatter_kernel(len_ref, q_ref, k_ref, v_ref, out_ref, ctx_buf, send_sem, recv_sem, own_sem):
    n_dev, chunk = out_ref.shape[0], out_ref.shape[1]
    me = lax.axis_index("seq")
    place = (lax.axis_index("doc_y"), lax.axis_index("doc_x"))
    barrier = pltpu.get_barrier_semaphore()

    def greet(t, carry):
        @pl.when(t != me)
        def _():
            pl.semaphore_signal(barrier, inc=1, device_id=place + (t,), device_id_type=MESH)

        return carry

    lax.fori_loop(0, n_dev, greet, 0)
    pl.semaphore_wait(barrier, n_dev - 1)
    length = len_ref[0]

    def block(b, carry):
        rows = pl.ds(pl.multiple_of(b * 2 * chunk, 2 * chunk), 2 * chunk)
        scores = lax.dot_general(
            q_ref[rows, :], k_ref[...], (((1,), (1,)), ((), ())), preferred_element_type=jnp.float32
        ) * HEAD_DIM ** (-0.5)
        key_pos = lax.broadcasted_iota(jnp.int32, scores.shape, 1)
        scores = jnp.where(key_pos < length, scores, -1e30)
        row_max = jnp.max(scores, axis=1, keepdims=True)
        weights = jnp.exp(scores - row_max)
        denominator = jnp.sum(weights, axis=1, keepdims=True)
        weighted = jnp.dot(weights.astype(jnp.bfloat16), v_ref[...], preferred_element_type=jnp.float32)
        context = (weighted / denominator).astype(jnp.bfloat16)
        ctx_buf[pl.ds(2 * b, 2)] = context.reshape(2, chunk, context.shape[1])
        for j in range(2):
            owner = 2 * b + j

            @pl.when(owner != me)
            def _():
                pltpu.make_async_remote_copy(
                    src_ref=ctx_buf.at[owner], dst_ref=out_ref.at[me], send_sem=send_sem, recv_sem=recv_sem,
                    device_id=place + (owner,), device_id_type=MESH,
                ).start()

        return carry

    lax.fori_loop(0, n_dev // 2, block, 0)
    own = pltpu.make_async_copy(ctx_buf.at[me], out_ref.at[me], own_sem)
    own.start()
    every = pltpu.make_async_remote_copy(
        src_ref=ctx_buf.at[pl.ds(0, n_dev - 1)], dst_ref=out_ref.at[pl.ds(0, n_dev - 1)], send_sem=send_sem,
        recv_sem=recv_sem, device_id=place + (me,), device_id_type=MESH,
    )
    every.wait_send()
    every.wait_recv()
    own.wait()


def attend_scatter(queries, keys_in, values_in, length, n_dev):
    nq, width = queries.shape
    chunk = nq // n_dev
    nk = keys_in.shape[0]
    vmem = pl.BlockSpec(memory_space=pltpu.VMEM)
    return pl.pallas_call(
        _attend_scatter_kernel,
        out_shape=jax.ShapeDtypeStruct((n_dev, chunk, width), jnp.bfloat16),
        in_specs=[pl.BlockSpec(memory_space=pltpu.SMEM), vmem, vmem, vmem],
        out_specs=pl.BlockSpec(memory_space=pl.ANY),
        scratch_shapes=[
            pltpu.VMEM((n_dev, chunk, width), jnp.bfloat16),
            pltpu.SemaphoreType.DMA,
            pltpu.SemaphoreType.DMA,
            pltpu.SemaphoreType.DMA,
        ],
        cost_estimate=pl.CostEstimate(
            flops=4 * nq * nk * width, transcendentals=nq * nk, bytes_accessed=2 * (2 * nq * width + 2 * nk * width)
        ),
        compiler_params=pltpu.CompilerParams(
            collective_id=1, has_side_effects=True, vmem_limit_bytes=48 * 1024 * 1024
        ),
    )(length.reshape(1), queries, keys_in, values_in)


def shards(enc_query, enc_key, enc_value, sum_query, doc_len, w_memory):
    length = doc_len[0]
    n_seq = lax.axis_size("seq")
    core = lax.axis_index("seq") % 2
    sibling = [(i, i ^ 1) for i in range(n_seq)]
    half = w_memory.shape[2] // 2
    w_half = lax.dynamic_slice_in_dim(w_memory, core * half, half, axis=2)
    w_pair = lax.ppermute(w_half, "doc_x", perm=[(0, 1), (1, 0)])
    w_half = jnp.where(lax.axis_index("doc_x") == 0, jnp.concatenate([w_half, w_pair], axis=2),
                       jnp.concatenate([w_pair, w_half], axis=2))
    w_half = lax.all_gather(w_half, "doc_y", axis=2, tiled=True)

    rows, sum_rows = enc_query.shape[1], sum_query.shape[1]
    mixed = lax.all_to_all(
        jnp.concatenate([enc_query[0], enc_key[0], enc_value[0], sum_query[0]], axis=0),
        "seq", split_axis=1, concat_axis=0, tiled=True,
    ).reshape(n_seq, 3 * rows + sum_rows, -1)
    head_query, head_key, head_value = (mixed[:, i * rows:(i + 1) * rows].reshape(n_seq * rows, -1) for i in range(3))
    summary_heads = mixed[:, 3 * rows:].reshape(n_seq * sum_rows, -1)
    by_head = attend_scatter(head_query, head_key, head_value, length, n_seq)
    encoder_out = by_head.transpose(1, 0, 2).reshape(by_head.shape[1], -1)

    enc_pair = jnp.concatenate([encoder_out, lax.ppermute(encoder_out, "seq", sibling)], axis=0)
    made = jnp.einsum("tf,kfc->ktc", enc_pair, w_half, preferred_element_type=jnp.float32).astype(jnp.bfloat16)
    made = made.reshape(2, 2, rows, -1, half).transpose(1, 3, 0, 2, 4)
    own, received = made[0], lax.ppermute(made[1], "seq", sibling)
    by_head = jnp.where(core == 0, jnp.stack([own, received], axis=1), jnp.stack([received, own], axis=1))
    by_head = by_head.reshape(n_seq, 2, rows, half)
    memory = lax.all_to_all(by_head, "seq", split_axis=0, concat_axis=2, tiled=True)
    memory_keys, memory_values = memory[0, 0], memory[0, 1]
    answer = attend_head(summary_heads, memory_keys, memory_values, length)
    summary_out = lax.all_to_all(answer, "seq", split_axis=0, concat_axis=1, tiled=True)
    return (encoder_out[None], summary_out[None])


def solution(mesh):
    n_doc = mesh.shape["doc"]
    split = jax.sharding.Mesh(mesh.devices.reshape(n_doc // 2, 2, mesh.shape["seq"]), ("doc_y", "doc_x", "seq"))
    doc = ("doc_y", "doc_x")
    in_specs = (
        P(doc, "seq", None),
        P(doc, "seq", None),
        P(doc, "seq", None),
        P(doc, "seq", None),
        P(doc),
        P(None, None, doc),
    )
    out_specs = (P(doc, "seq", None), P(doc, "seq", None))
    return jax.shard_map(shards, mesh=split, in_specs=in_specs, out_specs=out_specs, check_vma=False)
```

```python
import jax
import jax.numpy as jnp
from jax import lax
from jax.experimental import pallas as pl
from jax.experimental.pallas import tpu as pltpu
from jax.sharding import PartitionSpec as P

HEAD_DIM = 64


def _attend_kernel(len_ref, q_ref, k_ref, v_ref, o_ref):
    scores = lax.dot_general(
        q_ref[...], k_ref[...], (((1,), (1,)), ((), ())), preferred_element_type=jnp.float32
    ) * HEAD_DIM ** (-0.5)
    key_pos = lax.broadcasted_iota(jnp.int32, scores.shape, 1)
    scores = jnp.where(key_pos < len_ref[0], scores, -1e30)
    row_max = jnp.max(scores, axis=1, keepdims=True)
    weights = jnp.exp(scores - row_max)
    denominator = jnp.sum(weights, axis=1, keepdims=True)
    weighted = jnp.dot(weights.astype(jnp.bfloat16), v_ref[...], preferred_element_type=jnp.float32)
    o_ref[...] = (weighted / denominator).astype(o_ref.dtype)


def attend_head(queries, keys_in, values_in, length, block_rows=256):
    nq, width = queries.shape
    nk = keys_in.shape[0]
    block_rows = min(block_rows, nq)
    grid_spec = pltpu.PrefetchScalarGridSpec(
        num_scalar_prefetch=1,
        grid=(nq // block_rows,),
        in_specs=[
            pl.BlockSpec((block_rows, width), lambda i, n: (i, 0)),
            pl.BlockSpec((nk, width), lambda i, n: (0, 0)),
            pl.BlockSpec((nk, width), lambda i, n: (0, 0)),
        ],
        out_specs=pl.BlockSpec((block_rows, width), lambda i, n: (i, 0)),
    )
    cost = pl.CostEstimate(
        flops=4 * nq * nk * width,
        transcendentals=nq * nk,
        bytes_accessed=2 * (2 * nq * width + 2 * nk * width),
    )
    return pl.pallas_call(
        _attend_kernel,
        grid_spec=grid_spec,
        out_shape=jax.ShapeDtypeStruct((nq, width), jnp.bfloat16),
        cost_estimate=cost,
        compiler_params=pltpu.CompilerParams(vmem_limit_bytes=48 * 1024 * 1024),
    )(length.reshape(1), queries, keys_in, values_in)


MESH = pl.DeviceIdType.MESH


def _attend_scatter_kernel(len_ref, q_ref, k_ref, v_ref, out_ref, ctx_buf, send_sem, recv_sem, own_sem):
    n_dev, chunk = out_ref.shape[0], out_ref.shape[1]
    me = lax.axis_index("seq")
    place = (lax.axis_index("doc_y"), lax.axis_index("doc_x"))
    barrier = pltpu.get_barrier_semaphore()

    def greet(t, carry):
        @pl.when(t != me)
        def _():
            pl.semaphore_signal(barrier, inc=1, device_id=place + (t,), device_id_type=MESH)

        return carry

    lax.fori_loop(0, n_dev, greet, 0)
    pl.semaphore_wait(barrier, n_dev - 1)
    length = len_ref[0]

    def block(b, carry):
        rows = pl.ds(pl.multiple_of(b * 2 * chunk, 2 * chunk), 2 * chunk)
        scores = lax.dot_general(
            q_ref[rows, :], k_ref[...], (((1,), (1,)), ((), ())), preferred_element_type=jnp.float32
        ) * HEAD_DIM ** (-0.5)
        key_pos = lax.broadcasted_iota(jnp.int32, scores.shape, 1)
        scores = jnp.where(key_pos < length, scores, -1e30)
        row_max = jnp.max(scores, axis=1, keepdims=True)
        weights = jnp.exp(scores - row_max)
        denominator = jnp.sum(weights, axis=1, keepdims=True)
        weighted = jnp.dot(weights.astype(jnp.bfloat16), v_ref[...], preferred_element_type=jnp.float32)
        context = (weighted / denominator).astype(jnp.bfloat16)
        ctx_buf[pl.ds(2 * b, 2)] = context.reshape(2, chunk, context.shape[1])
        for j in range(2):
            owner = 2 * b + j

            @pl.when(owner != me)
            def _():
                pltpu.make_async_remote_copy(
                    src_ref=ctx_buf.at[owner], dst_ref=out_ref.at[me], send_sem=send_sem, recv_sem=recv_sem,
                    device_id=place + (owner,), device_id_type=MESH,
                ).start()

        return carry

    lax.fori_loop(0, n_dev // 2, block, 0)
    own = pltpu.make_async_copy(ctx_buf.at[me], out_ref.at[me], own_sem)
    own.start()
    every = pltpu.make_async_remote_copy(
        src_ref=ctx_buf.at[pl.ds(0, n_dev - 1)], dst_ref=out_ref.at[pl.ds(0, n_dev - 1)], send_sem=send_sem,
        recv_sem=recv_sem, device_id=place + (me,), device_id_type=MESH,
    )
    every.wait_send()
    every.wait_recv()
    own.wait()


def attend_scatter(queries, keys_in, values_in, length, n_dev):
    nq, width = queries.shape
    chunk = nq // n_dev
    nk = keys_in.shape[0]
    vmem = pl.BlockSpec(memory_space=pltpu.VMEM)
    return pl.pallas_call(
        _attend_scatter_kernel,
        out_shape=jax.ShapeDtypeStruct((n_dev, chunk, width), jnp.bfloat16),
        in_specs=[pl.BlockSpec(memory_space=pltpu.SMEM), vmem, vmem, vmem],
        out_specs=pl.BlockSpec(memory_space=pl.ANY),
        scratch_shapes=[
            pltpu.VMEM((n_dev, chunk, width), jnp.bfloat16),
            pltpu.SemaphoreType.DMA,
            pltpu.SemaphoreType.DMA,
            pltpu.SemaphoreType.DMA,
        ],
        cost_estimate=pl.CostEstimate(
            flops=4 * nq * nk * width, transcendentals=nq * nk, bytes_accessed=2 * (2 * nq * width + 2 * nk * width)
        ),
        compiler_params=pltpu.CompilerParams(
            collective_id=1, has_side_effects=True, vmem_limit_bytes=48 * 1024 * 1024
        ),
    )(length.reshape(1), queries, keys_in, values_in)


def _summary_kernel(len_ref, mem_ref, q_ref, out_ref, mem_in, ctx_buf, sems):
    n_dev, chunk = mem_ref.shape[0], mem_ref.shape[2]
    sum_chunk = out_ref.shape[1]
    me = lax.axis_index("seq")
    place = (lax.axis_index("doc_y"), lax.axis_index("doc_x"))
    barrier = pltpu.get_barrier_semaphore()

    def greet(t, carry):
        @pl.when(t != me)
        def _():
            pl.semaphore_signal(barrier, inc=1, device_id=place + (t,), device_id_type=MESH)

        return carry

    lax.fori_loop(0, n_dev, greet, 0)
    pl.semaphore_wait(barrier, n_dev - 1)

    def send_memory(t, carry):
        @pl.when(t != me)
        def _():
            pltpu.make_async_remote_copy(
                src_ref=mem_ref.at[t], dst_ref=mem_in.at[me], send_sem=sems.at[0], recv_sem=sems.at[1],
                device_id=place + (t,), device_id_type=MESH,
            ).start()

        return carry

    lax.fori_loop(0, n_dev, send_memory, 0)
    own = pltpu.make_async_copy(mem_ref.at[me], mem_in.at[me], sems.at[2])
    own.start()
    every = pltpu.make_async_remote_copy(
        src_ref=mem_ref.at[pl.ds(0, n_dev - 1)], dst_ref=mem_in.at[pl.ds(0, n_dev - 1)], send_sem=sems.at[0],
        recv_sem=sems.at[1], device_id=place + (me,), device_id_type=MESH,
    )
    every.wait_recv()
    own.wait()

    keys = mem_in[:, 0].reshape(n_dev * chunk, -1)
    values = mem_in[:, 1].reshape(n_dev * chunk, -1)
    scores = lax.dot_general(
        q_ref[...], keys, (((1,), (1,)), ((), ())), preferred_element_type=jnp.float32
    ) * HEAD_DIM ** (-0.5)
    key_pos = lax.broadcasted_iota(jnp.int32, scores.shape, 1)
    scores = jnp.where(key_pos < len_ref[0], scores, -1e30)
    row_max = jnp.max(scores, axis=1, keepdims=True)
    weights = jnp.exp(scores - row_max)
    denominator = jnp.sum(weights, axis=1, keepdims=True)
    weighted = jnp.dot(weights.astype(jnp.bfloat16), values, preferred_element_type=jnp.float32)
    context = (weighted / denominator).astype(jnp.bfloat16)
    ctx_buf[...] = context.reshape(n_dev, sum_chunk, context.shape[1])

    def send_context(t, carry):
        @pl.when(t != me)
        def _():
            pltpu.make_async_remote_copy(
                src_ref=ctx_buf.at[t], dst_ref=out_ref.at[me], send_sem=sems.at[3], recv_sem=sems.at[4],
                device_id=place + (t,), device_id_type=MESH,
            ).start()

        return carry

    lax.fori_loop(0, n_dev, send_context, 0)
    back = pltpu.make_async_copy(ctx_buf.at[me], out_ref.at[me], sems.at[5])
    back.start()
    every.wait_send()
    returned = pltpu.make_async_remote_copy(
        src_ref=ctx_buf.at[pl.ds(0, n_dev - 1)], dst_ref=out_ref.at[pl.ds(0, n_dev - 1)], send_sem=sems.at[3],
        recv_sem=sems.at[4], device_id=place + (me,), device_id_type=MESH,
    )
    returned.wait_send()
    returned.wait_recv()
    back.wait()


def summary_exchange(memory_by_head, summary_queries, length):
    n_dev, _, chunk, width = memory_by_head.shape
    nq = summary_queries.shape[0]
    vmem = pl.BlockSpec(memory_space=pltpu.VMEM)
    return pl.pallas_call(
        _summary_kernel,
        out_shape=jax.ShapeDtypeStruct((n_dev, nq // n_dev, width), jnp.bfloat16),
        in_specs=[pl.BlockSpec(memory_space=pltpu.SMEM), vmem, vmem],
        out_specs=pl.BlockSpec(memory_space=pl.ANY),
        scratch_shapes=[
            pltpu.VMEM(memory_by_head.shape, jnp.bfloat16),
            pltpu.VMEM((n_dev, nq // n_dev, width), jnp.bfloat16),
            pltpu.SemaphoreType.DMA((6,)),
        ],
        cost_estimate=pl.CostEstimate(
            flops=4 * nq * n_dev * chunk * width, transcendentals=nq * n_dev * chunk,
            bytes_accessed=2 * (2 * nq * width + 2 * n_dev * chunk * width),
        ),
        compiler_params=pltpu.CompilerParams(
            collective_id=2, has_side_effects=True, vmem_limit_bytes=48 * 1024 * 1024
        ),
    )(length.reshape(1), memory_by_head, summary_queries)


def shards(enc_query, enc_key, enc_value, sum_query, doc_len, w_memory):
    length = doc_len[0]
    n_seq = lax.axis_size("seq")
    core = lax.axis_index("seq") % 2
    sibling = [(i, i ^ 1) for i in range(n_seq)]
    half = w_memory.shape[2] // 2
    w_half = lax.dynamic_slice_in_dim(w_memory, core * half, half, axis=2)
    w_pair = lax.ppermute(w_half, "doc_x", perm=[(0, 1), (1, 0)])
    w_half = jnp.where(lax.axis_index("doc_x") == 0, jnp.concatenate([w_half, w_pair], axis=2),
                       jnp.concatenate([w_pair, w_half], axis=2))
    w_half = lax.all_gather(w_half, "doc_y", axis=2, tiled=True)

    rows, sum_rows = enc_query.shape[1], sum_query.shape[1]
    mixed = lax.all_to_all(
        jnp.concatenate([enc_query[0], enc_key[0], enc_value[0], sum_query[0]], axis=0),
        "seq", split_axis=1, concat_axis=0, tiled=True,
    ).reshape(n_seq, 3 * rows + sum_rows, -1)
    head_query, head_key, head_value = (mixed[:, i * rows:(i + 1) * rows].reshape(n_seq * rows, -1) for i in range(3))
    summary_heads = mixed[:, 3 * rows:].reshape(n_seq * sum_rows, -1)
    by_head = attend_scatter(head_query, head_key, head_value, length, n_seq)
    encoder_out = by_head.transpose(1, 0, 2).reshape(by_head.shape[1], -1)

    enc_pair = jnp.concatenate([encoder_out, lax.ppermute(encoder_out, "seq", sibling)], axis=0)
    made = jnp.einsum("tf,kfc->ktc", enc_pair, w_half, preferred_element_type=jnp.float32).astype(jnp.bfloat16)
    made = made.reshape(2, 2, rows, -1, half).transpose(1, 3, 0, 2, 4)
    own, received = made[0], lax.ppermute(made[1], "seq", sibling)
    by_head = jnp.where(core == 0, jnp.stack([own, received], axis=1), jnp.stack([received, own], axis=1))
    by_head = by_head.reshape(n_seq, 2, rows, half)
    answer = summary_exchange(by_head, summary_heads, length)
    summary_out = answer.transpose(1, 0, 2).reshape(answer.shape[1], -1)
    return (encoder_out[None], summary_out[None])


def solution(mesh):
    n_doc = mesh.shape["doc"]
    split = jax.sharding.Mesh(mesh.devices.reshape(n_doc // 2, 2, mesh.shape["seq"]), ("doc_y", "doc_x", "seq"))
    doc = ("doc_y", "doc_x")
    in_specs = (
        P(doc, "seq", None),
        P(doc, "seq", None),
        P(doc, "seq", None),
        P(doc, "seq", None),
        P(doc),
        P(None, None, doc),
    )
    out_specs = (P(doc, "seq", None), P(doc, "seq", None))
    return jax.shard_map(shards, mesh=split, in_specs=in_specs, out_specs=out_specs, check_vma=False)
```

```python
import jax
import jax.numpy as jnp
from jax import lax
from jax.experimental import pallas as pl
from jax.experimental.pallas import tpu as pltpu
from jax.sharding import PartitionSpec as P

HEAD_DIM = 64


def _attend_kernel(len_ref, q_ref, k_ref, v_ref, o_ref):
    scores = lax.dot_general(
        q_ref[...], k_ref[...], (((1,), (1,)), ((), ())), preferred_element_type=jnp.float32
    ) * HEAD_DIM ** (-0.5)
    key_pos = lax.broadcasted_iota(jnp.int32, scores.shape, 1)
    scores = jnp.where(key_pos < len_ref[0], scores, -1e30)
    row_max = jnp.max(scores, axis=1, keepdims=True)
    weights = jnp.exp(scores - row_max)
    denominator = jnp.sum(weights, axis=1, keepdims=True)
    weighted = jnp.dot(weights.astype(jnp.bfloat16), v_ref[...], preferred_element_type=jnp.float32)
    o_ref[...] = (weighted / denominator).astype(o_ref.dtype)


def attend_head(queries, keys_in, values_in, length, block_rows=256):
    nq, width = queries.shape
    nk = keys_in.shape[0]
    block_rows = min(block_rows, nq)
    grid_spec = pltpu.PrefetchScalarGridSpec(
        num_scalar_prefetch=1,
        grid=(nq // block_rows,),
        in_specs=[
            pl.BlockSpec((block_rows, width), lambda i, n: (i, 0)),
            pl.BlockSpec((nk, width), lambda i, n: (0, 0)),
            pl.BlockSpec((nk, width), lambda i, n: (0, 0)),
        ],
        out_specs=pl.BlockSpec((block_rows, width), lambda i, n: (i, 0)),
    )
    cost = pl.CostEstimate(
        flops=4 * nq * nk * width,
        transcendentals=nq * nk,
        bytes_accessed=2 * (2 * nq * width + 2 * nk * width),
    )
    return pl.pallas_call(
        _attend_kernel,
        grid_spec=grid_spec,
        out_shape=jax.ShapeDtypeStruct((nq, width), jnp.bfloat16),
        cost_estimate=cost,
        compiler_params=pltpu.CompilerParams(vmem_limit_bytes=48 * 1024 * 1024),
    )(length.reshape(1), queries, keys_in, values_in)


MESH = pl.DeviceIdType.MESH


def _attend_scatter_kernel(len_ref, q_ref, k_ref, v_ref, out_ref, ctx_buf, send_sem, recv_sem, own_sem):
    n_dev, chunk = out_ref.shape[0], out_ref.shape[1]
    me = lax.axis_index("seq")
    place = (lax.axis_index("doc_y"), lax.axis_index("doc_x"))
    barrier = pltpu.get_barrier_semaphore()

    def greet(t, carry):
        @pl.when(t != me)
        def _():
            pl.semaphore_signal(barrier, inc=1, device_id=place + (t,), device_id_type=MESH)

        return carry

    lax.fori_loop(0, n_dev, greet, 0)
    pl.semaphore_wait(barrier, n_dev - 1)
    length = len_ref[0]

    def block(step, carry):
        b = lax.rem(step + me // 2, n_dev // 2)
        rows = pl.ds(pl.multiple_of(b * 2 * chunk, 2 * chunk), 2 * chunk)
        scores = lax.dot_general(
            q_ref[rows, :], k_ref[...], (((1,), (1,)), ((), ())), preferred_element_type=jnp.float32
        ) * HEAD_DIM ** (-0.5)
        key_pos = lax.broadcasted_iota(jnp.int32, scores.shape, 1)
        scores = jnp.where(key_pos < length, scores, -1e30)
        row_max = jnp.max(scores, axis=1, keepdims=True)
        weights = jnp.exp(scores - row_max)
        denominator = jnp.sum(weights, axis=1, keepdims=True)
        weighted = jnp.dot(weights.astype(jnp.bfloat16), v_ref[...], preferred_element_type=jnp.float32)
        context = (weighted / denominator).astype(jnp.bfloat16)
        ctx_buf[pl.ds(2 * b, 2)] = context.reshape(2, chunk, context.shape[1])
        for j in range(2):
            owner = 2 * b + j

            @pl.when(owner != me)
            def _():
                pltpu.make_async_remote_copy(
                    src_ref=ctx_buf.at[owner], dst_ref=out_ref.at[me], send_sem=send_sem, recv_sem=recv_sem,
                    device_id=place + (owner,), device_id_type=MESH,
                ).start()

        return carry

    lax.fori_loop(0, n_dev // 2, block, 0)
    own = pltpu.make_async_copy(ctx_buf.at[me], out_ref.at[me], own_sem)
    own.start()
    every = pltpu.make_async_remote_copy(
        src_ref=ctx_buf.at[pl.ds(0, n_dev - 1)], dst_ref=out_ref.at[pl.ds(0, n_dev - 1)], send_sem=send_sem,
        recv_sem=recv_sem, device_id=place + (me,), device_id_type=MESH,
    )
    every.wait_send()
    every.wait_recv()
    own.wait()


def attend_scatter(queries, keys_in, values_in, length, n_dev):
    nq, width = queries.shape
    chunk = nq // n_dev
    nk = keys_in.shape[0]
    vmem = pl.BlockSpec(memory_space=pltpu.VMEM)
    return pl.pallas_call(
        _attend_scatter_kernel,
        out_shape=jax.ShapeDtypeStruct((n_dev, chunk, width), jnp.bfloat16),
        in_specs=[pl.BlockSpec(memory_space=pltpu.SMEM), vmem, vmem, vmem],
        out_specs=pl.BlockSpec(memory_space=pl.ANY),
        scratch_shapes=[
            pltpu.VMEM((n_dev, chunk, width), jnp.bfloat16),
            pltpu.SemaphoreType.DMA,
            pltpu.SemaphoreType.DMA,
            pltpu.SemaphoreType.DMA,
        ],
        cost_estimate=pl.CostEstimate(
            flops=4 * nq * nk * width, transcendentals=nq * nk, bytes_accessed=2 * (2 * nq * width + 2 * nk * width)
        ),
        compiler_params=pltpu.CompilerParams(
            collective_id=1, has_side_effects=True, vmem_limit_bytes=48 * 1024 * 1024
        ),
    )(length.reshape(1), queries, keys_in, values_in)


def _summary_kernel(len_ref, mem_ref, q_ref, out_ref, mem_in, ctx_buf, sems):
    n_dev, chunk = mem_ref.shape[0], mem_ref.shape[2]
    sum_chunk = out_ref.shape[1]
    me = lax.axis_index("seq")
    place = (lax.axis_index("doc_y"), lax.axis_index("doc_x"))
    barrier = pltpu.get_barrier_semaphore()

    def greet(t, carry):
        @pl.when(t != me)
        def _():
            pl.semaphore_signal(barrier, inc=1, device_id=place + (t,), device_id_type=MESH)

        return carry

    lax.fori_loop(0, n_dev, greet, 0)
    pl.semaphore_wait(barrier, n_dev - 1)

    def send_memory(step, carry):
        t = lax.rem(me + step, n_dev)
        pltpu.make_async_remote_copy(
            src_ref=mem_ref.at[t], dst_ref=mem_in.at[me], send_sem=sems.at[0], recv_sem=sems.at[1],
            device_id=place + (t,), device_id_type=MESH,
        ).start()
        return carry

    lax.fori_loop(1, n_dev, send_memory, 0)
    own = pltpu.make_async_copy(mem_ref.at[me], mem_in.at[me], sems.at[2])
    own.start()
    every = pltpu.make_async_remote_copy(
        src_ref=mem_ref.at[pl.ds(0, n_dev - 1)], dst_ref=mem_in.at[pl.ds(0, n_dev - 1)], send_sem=sems.at[0],
        recv_sem=sems.at[1], device_id=place + (me,), device_id_type=MESH,
    )
    every.wait_recv()
    own.wait()

    keys = mem_in[:, 0].reshape(n_dev * chunk, -1)
    values = mem_in[:, 1].reshape(n_dev * chunk, -1)
    scores = lax.dot_general(
        q_ref[...], keys, (((1,), (1,)), ((), ())), preferred_element_type=jnp.float32
    ) * HEAD_DIM ** (-0.5)
    key_pos = lax.broadcasted_iota(jnp.int32, scores.shape, 1)
    scores = jnp.where(key_pos < len_ref[0], scores, -1e30)
    row_max = jnp.max(scores, axis=1, keepdims=True)
    weights = jnp.exp(scores - row_max)
    denominator = jnp.sum(weights, axis=1, keepdims=True)
    weighted = jnp.dot(weights.astype(jnp.bfloat16), values, preferred_element_type=jnp.float32)
    context = (weighted / denominator).astype(jnp.bfloat16)
    ctx_buf[...] = context.reshape(n_dev, sum_chunk, context.shape[1])

    def send_context(step, carry):
        t = lax.rem(me + step, n_dev)
        pltpu.make_async_remote_copy(
            src_ref=ctx_buf.at[t], dst_ref=out_ref.at[me], send_sem=sems.at[3], recv_sem=sems.at[4],
            device_id=place + (t,), device_id_type=MESH,
        ).start()
        return carry

    lax.fori_loop(1, n_dev, send_context, 0)
    back = pltpu.make_async_copy(ctx_buf.at[me], out_ref.at[me], sems.at[5])
    back.start()
    every.wait_send()
    returned = pltpu.make_async_remote_copy(
        src_ref=ctx_buf.at[pl.ds(0, n_dev - 1)], dst_ref=out_ref.at[pl.ds(0, n_dev - 1)], send_sem=sems.at[3],
        recv_sem=sems.at[4], device_id=place + (me,), device_id_type=MESH,
    )
    returned.wait_send()
    returned.wait_recv()
    back.wait()


def summary_exchange(memory_by_head, summary_queries, length):
    n_dev, _, chunk, width = memory_by_head.shape
    nq = summary_queries.shape[0]
    vmem = pl.BlockSpec(memory_space=pltpu.VMEM)
    return pl.pallas_call(
        _summary_kernel,
        out_shape=jax.ShapeDtypeStruct((n_dev, nq // n_dev, width), jnp.bfloat16),
        in_specs=[pl.BlockSpec(memory_space=pltpu.SMEM), vmem, vmem],
        out_specs=pl.BlockSpec(memory_space=pl.ANY),
        scratch_shapes=[
            pltpu.VMEM(memory_by_head.shape, jnp.bfloat16),
            pltpu.VMEM((n_dev, nq // n_dev, width), jnp.bfloat16),
            pltpu.SemaphoreType.DMA((6,)),
        ],
        cost_estimate=pl.CostEstimate(
            flops=4 * nq * n_dev * chunk * width, transcendentals=nq * n_dev * chunk,
            bytes_accessed=2 * (2 * nq * width + 2 * n_dev * chunk * width),
        ),
        compiler_params=pltpu.CompilerParams(
            collective_id=2, has_side_effects=True, vmem_limit_bytes=48 * 1024 * 1024
        ),
    )(length.reshape(1), memory_by_head, summary_queries)


def shards(enc_query, enc_key, enc_value, sum_query, doc_len, w_memory):
    length = doc_len[0]
    n_seq = lax.axis_size("seq")
    core = lax.axis_index("seq") % 2
    sibling = [(i, i ^ 1) for i in range(n_seq)]
    half = w_memory.shape[2] // 2
    w_half = lax.dynamic_slice_in_dim(w_memory, core * half, half, axis=2)
    w_pair = lax.ppermute(w_half, "doc_x", perm=[(0, 1), (1, 0)])
    w_half = jnp.where(lax.axis_index("doc_x") == 0, jnp.concatenate([w_half, w_pair], axis=2),
                       jnp.concatenate([w_pair, w_half], axis=2))
    w_half = lax.all_gather(w_half, "doc_y", axis=2, tiled=True)

    rows, sum_rows = enc_query.shape[1], sum_query.shape[1]
    mixed = lax.all_to_all(
        jnp.concatenate([enc_query[0], enc_key[0], enc_value[0], sum_query[0]], axis=0),
        "seq", split_axis=1, concat_axis=0, tiled=True,
    ).reshape(n_seq, 3 * rows + sum_rows, -1)
    head_query, head_key, head_value = (mixed[:, i * rows:(i + 1) * rows].reshape(n_seq * rows, -1) for i in range(3))
    summary_heads = mixed[:, 3 * rows:].reshape(n_seq * sum_rows, -1)
    by_head = attend_scatter(head_query, head_key, head_value, length, n_seq)
    encoder_out = by_head.transpose(1, 0, 2).reshape(by_head.shape[1], -1)

    enc_pair = jnp.concatenate([encoder_out, lax.ppermute(encoder_out, "seq", sibling)], axis=0)
    made = jnp.einsum("tf,kfc->ktc", enc_pair, w_half, preferred_element_type=jnp.float32).astype(jnp.bfloat16)
    made = made.reshape(2, 2, rows, -1, half).transpose(1, 3, 0, 2, 4)
    own, received = made[0], lax.ppermute(made[1], "seq", sibling)
    by_head = jnp.where(core == 0, jnp.stack([own, received], axis=1), jnp.stack([received, own], axis=1))
    by_head = by_head.reshape(n_seq, 2, rows, half)
    answer = summary_exchange(by_head, summary_heads, length)
    summary_out = answer.transpose(1, 0, 2).reshape(answer.shape[1], -1)
    return (encoder_out[None], summary_out[None])


def solution(mesh):
    n_doc = mesh.shape["doc"]
    split = jax.sharding.Mesh(mesh.devices.reshape(n_doc // 2, 2, mesh.shape["seq"]), ("doc_y", "doc_x", "seq"))
    doc = ("doc_y", "doc_x")
    in_specs = (
        P(doc, "seq", None),
        P(doc, "seq", None),
        P(doc, "seq", None),
        P(doc, "seq", None),
        P(doc),
        P(None, None, doc),
    )
    out_specs = (P(doc, "seq", None), P(doc, "seq", None))
    return jax.shard_map(shards, mesh=split, in_specs=in_specs, out_specs=out_specs, check_vma=False)
```

```python
import jax
import jax.numpy as jnp
from jax import lax
from jax.experimental import pallas as pl
from jax.experimental.pallas import tpu as pltpu
from jax.sharding import PartitionSpec as P

HEAD_DIM = 64


def _attend_kernel(len_ref, q_ref, k_ref, v_ref, o_ref):
    scores = lax.dot_general(
        q_ref[...], k_ref[...], (((1,), (1,)), ((), ())), preferred_element_type=jnp.float32
    ) * HEAD_DIM ** (-0.5)
    key_pos = lax.broadcasted_iota(jnp.int32, scores.shape, 1)
    scores = jnp.where(key_pos < len_ref[0], scores, -1e30)
    row_max = jnp.max(scores, axis=1, keepdims=True)
    weights = jnp.exp(scores - row_max)
    denominator = jnp.sum(weights, axis=1, keepdims=True)
    weighted = jnp.dot(weights.astype(jnp.bfloat16), v_ref[...], preferred_element_type=jnp.float32)
    o_ref[...] = (weighted / denominator).astype(o_ref.dtype)


def attend_head(queries, keys_in, values_in, length, block_rows=256):
    nq, width = queries.shape
    nk = keys_in.shape[0]
    block_rows = min(block_rows, nq)
    grid_spec = pltpu.PrefetchScalarGridSpec(
        num_scalar_prefetch=1,
        grid=(nq // block_rows,),
        in_specs=[
            pl.BlockSpec((block_rows, width), lambda i, n: (i, 0)),
            pl.BlockSpec((nk, width), lambda i, n: (0, 0)),
            pl.BlockSpec((nk, width), lambda i, n: (0, 0)),
        ],
        out_specs=pl.BlockSpec((block_rows, width), lambda i, n: (i, 0)),
    )
    cost = pl.CostEstimate(
        flops=4 * nq * nk * width,
        transcendentals=nq * nk,
        bytes_accessed=2 * (2 * nq * width + 2 * nk * width),
    )
    return pl.pallas_call(
        _attend_kernel,
        grid_spec=grid_spec,
        out_shape=jax.ShapeDtypeStruct((nq, width), jnp.bfloat16),
        cost_estimate=cost,
        compiler_params=pltpu.CompilerParams(vmem_limit_bytes=48 * 1024 * 1024),
    )(length.reshape(1), queries, keys_in, values_in)


MESH = pl.DeviceIdType.MESH


def _attend_scatter_kernel(len_ref, q_ref, k_ref, v_ref, out_ref, ctx_buf, send_sem, recv_sem, own_sem):
    n_dev, chunk = out_ref.shape[0], out_ref.shape[1]
    me = lax.axis_index("seq")
    place = (lax.axis_index("doc_y"), lax.axis_index("doc_x"))
    barrier = pltpu.get_barrier_semaphore()

    def greet(t, carry):
        @pl.when(t != me)
        def _():
            pl.semaphore_signal(barrier, inc=1, device_id=place + (t,), device_id_type=MESH)

        return carry

    lax.fori_loop(0, n_dev, greet, 0)
    pl.semaphore_wait(barrier, n_dev - 1)
    length = len_ref[0]

    def block(step, carry):
        b = lax.rem(step + me // 2, n_dev // 2)
        rows = pl.ds(pl.multiple_of(b * 2 * chunk, 2 * chunk), 2 * chunk)
        scores = lax.dot_general(
            q_ref[rows, :], k_ref[...], (((1,), (1,)), ((), ())), preferred_element_type=jnp.float32
        ) * HEAD_DIM ** (-0.5)
        key_pos = lax.broadcasted_iota(jnp.int32, scores.shape, 1)
        scores = jnp.where(key_pos < length, scores, -1e30)
        row_max = jnp.max(scores, axis=1, keepdims=True)
        weights = jnp.exp(scores - row_max)
        denominator = jnp.sum(weights, axis=1, keepdims=True)
        weighted = jnp.dot(weights.astype(jnp.bfloat16), v_ref[...], preferred_element_type=jnp.float32)
        context = (weighted / denominator).astype(jnp.bfloat16)
        ctx_buf[pl.ds(2 * b, 2)] = context.reshape(2, chunk, context.shape[1])
        for j in range(2):
            owner = 2 * b + j

            @pl.when(owner != me)
            def _():
                pltpu.make_async_remote_copy(
                    src_ref=ctx_buf.at[owner], dst_ref=out_ref.at[me], send_sem=send_sem, recv_sem=recv_sem,
                    device_id=place + (owner,), device_id_type=MESH,
                ).start()

        return carry

    lax.fori_loop(0, n_dev // 2, block, 0)
    own = pltpu.make_async_copy(ctx_buf.at[me], out_ref.at[me], own_sem)
    own.start()
    every = pltpu.make_async_remote_copy(
        src_ref=ctx_buf.at[pl.ds(0, n_dev - 1)], dst_ref=out_ref.at[pl.ds(0, n_dev - 1)], send_sem=send_sem,
        recv_sem=recv_sem, device_id=place + (me,), device_id_type=MESH,
    )
    every.wait_send()
    every.wait_recv()
    own.wait()


def attend_scatter(queries, keys_in, values_in, length, n_dev):
    nq, width = queries.shape
    chunk = nq // n_dev
    nk = keys_in.shape[0]
    vmem = pl.BlockSpec(memory_space=pltpu.VMEM)
    return pl.pallas_call(
        _attend_scatter_kernel,
        out_shape=jax.ShapeDtypeStruct((n_dev, chunk, width), jnp.bfloat16),
        in_specs=[pl.BlockSpec(memory_space=pltpu.SMEM), vmem, vmem, vmem],
        out_specs=pl.BlockSpec(memory_space=pl.ANY),
        scratch_shapes=[
            pltpu.VMEM((n_dev, chunk, width), jnp.bfloat16),
            pltpu.SemaphoreType.DMA,
            pltpu.SemaphoreType.DMA,
            pltpu.SemaphoreType.DMA,
        ],
        cost_estimate=pl.CostEstimate(
            flops=4 * nq * nk * width, transcendentals=nq * nk, bytes_accessed=2 * (2 * nq * width + 2 * nk * width)
        ),
        compiler_params=pltpu.CompilerParams(
            collective_id=1, has_side_effects=True, vmem_limit_bytes=48 * 1024 * 1024
        ),
    )(length.reshape(1), queries, keys_in, values_in)


def shards(enc_query, enc_key, enc_value, sum_query, doc_len, w_memory):
    length = doc_len[0]
    n_seq = lax.axis_size("seq")
    core = lax.axis_index("seq") % 2
    sibling = [(i, i ^ 1) for i in range(n_seq)]
    half = w_memory.shape[2] // 2
    w_half = lax.dynamic_slice_in_dim(w_memory, core * half, half, axis=2)
    w_pair = lax.ppermute(w_half, "doc_x", perm=[(0, 1), (1, 0)])
    w_half = jnp.where(lax.axis_index("doc_x") == 0, jnp.concatenate([w_half, w_pair], axis=2),
                       jnp.concatenate([w_pair, w_half], axis=2))
    w_half = lax.all_gather(w_half, "doc_y", axis=2, tiled=True)

    rows, sum_rows = enc_query.shape[1], sum_query.shape[1]
    mixed = lax.all_to_all(
        jnp.concatenate([enc_query[0], enc_key[0], enc_value[0], sum_query[0]], axis=0),
        "seq", split_axis=1, concat_axis=0, tiled=True,
    ).reshape(n_seq, 3 * rows + sum_rows, -1)
    head_query, head_key, head_value = (mixed[:, i * rows:(i + 1) * rows].reshape(n_seq * rows, -1) for i in range(3))
    summary_heads = mixed[:, 3 * rows:].reshape(n_seq * sum_rows, -1)
    by_head = attend_scatter(head_query, head_key, head_value, length, n_seq)
    encoder_out = by_head.transpose(1, 0, 2).reshape(by_head.shape[1], -1)

    enc_pair = jnp.concatenate([encoder_out, lax.ppermute(encoder_out, "seq", sibling)], axis=0)
    made = jnp.einsum("tf,kfc->ktc", enc_pair, w_half, preferred_element_type=jnp.float32).astype(jnp.bfloat16)
    made = made.reshape(2, 2, rows, -1, half).transpose(1, 3, 0, 2, 4)
    own, received = made[0], lax.ppermute(made[1], "seq", sibling)
    by_head = jnp.where(core == 0, jnp.stack([own, received], axis=1), jnp.stack([received, own], axis=1))
    by_head = by_head.reshape(n_seq, 2, rows, half)
    memory = lax.all_to_all(by_head, "seq", split_axis=0, concat_axis=2, tiled=True)
    memory_keys, memory_values = memory[0, 0], memory[0, 1]
    answer = attend_head(summary_heads, memory_keys, memory_values, length)
    summary_out = lax.all_to_all(answer, "seq", split_axis=0, concat_axis=1, tiled=True)
    return (encoder_out[None], summary_out[None])


def solution(mesh):
    n_doc = mesh.shape["doc"]
    split = jax.sharding.Mesh(mesh.devices.reshape(n_doc // 2, 2, mesh.shape["seq"]), ("doc_y", "doc_x", "seq"))
    doc = ("doc_y", "doc_x")
    in_specs = (
        P(doc, "seq", None),
        P(doc, "seq", None),
        P(doc, "seq", None),
        P(doc, "seq", None),
        P(doc),
        P(None, None, doc),
    )
    out_specs = (P(doc, "seq", None), P(doc, "seq", None))
    return jax.shard_map(shards, mesh=split, in_specs=in_specs, out_specs=out_specs, check_vma=False)
```

```python
import jax
import jax.numpy as jnp
from jax import lax
from jax.experimental import pallas as pl
from jax.experimental.pallas import tpu as pltpu
from jax.sharding import PartitionSpec as P

HEAD_DIM = 64


def _attend_kernel(len_ref, q_ref, k_ref, v_ref, o_ref):
    scores = lax.dot_general(
        q_ref[...], k_ref[...], (((1,), (1,)), ((), ())), preferred_element_type=jnp.float32
    ) * HEAD_DIM ** (-0.5)
    key_pos = lax.broadcasted_iota(jnp.int32, scores.shape, 1)
    scores = jnp.where(key_pos < len_ref[0], scores, -1e30)
    row_max = jnp.max(scores, axis=1, keepdims=True)
    weights = jnp.exp(scores - row_max)
    denominator = jnp.sum(weights, axis=1, keepdims=True)
    weighted = jnp.dot(weights.astype(jnp.bfloat16), v_ref[...], preferred_element_type=jnp.float32)
    o_ref[...] = (weighted / denominator).astype(o_ref.dtype)


def attend_head(queries, keys_in, values_in, length, block_rows=256):
    nq, width = queries.shape
    nk = keys_in.shape[0]
    block_rows = min(block_rows, nq)
    grid_spec = pltpu.PrefetchScalarGridSpec(
        num_scalar_prefetch=1,
        grid=(nq // block_rows,),
        in_specs=[
            pl.BlockSpec((block_rows, width), lambda i, n: (i, 0)),
            pl.BlockSpec((nk, width), lambda i, n: (0, 0)),
            pl.BlockSpec((nk, width), lambda i, n: (0, 0)),
        ],
        out_specs=pl.BlockSpec((block_rows, width), lambda i, n: (i, 0)),
    )
    cost = pl.CostEstimate(
        flops=4 * nq * nk * width,
        transcendentals=nq * nk,
        bytes_accessed=2 * (2 * nq * width + 2 * nk * width),
    )
    return pl.pallas_call(
        _attend_kernel,
        grid_spec=grid_spec,
        out_shape=jax.ShapeDtypeStruct((nq, width), jnp.bfloat16),
        cost_estimate=cost,
        compiler_params=pltpu.CompilerParams(vmem_limit_bytes=48 * 1024 * 1024),
    )(length.reshape(1), queries, keys_in, values_in)


MESH = pl.DeviceIdType.MESH


def _attend_scatter_kernel(len_ref, q_ref, k_ref, v_ref, out_ref, ctx_buf, send_sem, recv_sem, own_sem):
    n_dev, chunk = out_ref.shape[0], out_ref.shape[1]
    me = lax.axis_index("seq")
    place = (lax.axis_index("doc_y"), lax.axis_index("doc_x"))
    barrier = pltpu.get_barrier_semaphore()

    def greet(t, carry):
        @pl.when(t != me)
        def _():
            pl.semaphore_signal(barrier, inc=1, device_id=place + (t,), device_id_type=MESH)

        return carry

    lax.fori_loop(0, n_dev, greet, 0)
    pl.semaphore_wait(barrier, n_dev - 1)
    length = len_ref[0]

    def block(step, carry):
        b = lax.rem(step + me // 2, n_dev // 2)
        rows = pl.ds(pl.multiple_of(b * 2 * chunk, 2 * chunk), 2 * chunk)
        scores = lax.dot_general(
            q_ref[rows, :], k_ref[...], (((1,), (1,)), ((), ())), preferred_element_type=jnp.float32
        ) * HEAD_DIM ** (-0.5)
        key_pos = lax.broadcasted_iota(jnp.int32, scores.shape, 1)
        scores = jnp.where(key_pos < length, scores, -1e30)
        row_max = jnp.max(scores, axis=1, keepdims=True)
        weights = jnp.exp(scores - row_max)
        denominator = jnp.sum(weights, axis=1, keepdims=True)
        weighted = jnp.dot(weights.astype(jnp.bfloat16), v_ref[...], preferred_element_type=jnp.float32)
        context = (weighted / denominator).astype(jnp.bfloat16)
        ctx_buf[pl.ds(2 * b, 2)] = context.reshape(2, chunk, context.shape[1])
        for j in range(2):
            owner = 2 * b + j

            @pl.when(owner != me)
            def _():
                pltpu.make_async_remote_copy(
                    src_ref=ctx_buf.at[owner], dst_ref=out_ref.at[me], send_sem=send_sem, recv_sem=recv_sem,
                    device_id=place + (owner,), device_id_type=MESH,
                ).start()

        return carry

    lax.fori_loop(0, n_dev // 2, block, 0)
    own = pltpu.make_async_copy(ctx_buf.at[me], out_ref.at[me], own_sem)
    own.start()
    every = pltpu.make_async_remote_copy(
        src_ref=ctx_buf.at[pl.ds(0, n_dev - 1)], dst_ref=out_ref.at[pl.ds(0, n_dev - 1)], send_sem=send_sem,
        recv_sem=recv_sem, device_id=place + (me,), device_id_type=MESH,
    )
    every.wait_send()
    every.wait_recv()
    own.wait()


def attend_scatter(queries, keys_in, values_in, length, n_dev, collective_id):
    nq, width = queries.shape
    chunk = nq // n_dev
    nk = keys_in.shape[0]
    vmem = pl.BlockSpec(memory_space=pltpu.VMEM)
    return pl.pallas_call(
        _attend_scatter_kernel,
        out_shape=jax.ShapeDtypeStruct((n_dev, chunk, width), jnp.bfloat16),
        in_specs=[pl.BlockSpec(memory_space=pltpu.SMEM), vmem, vmem, vmem],
        out_specs=pl.BlockSpec(memory_space=pl.ANY),
        scratch_shapes=[
            pltpu.VMEM((n_dev, chunk, width), jnp.bfloat16),
            pltpu.SemaphoreType.DMA,
            pltpu.SemaphoreType.DMA,
            pltpu.SemaphoreType.DMA,
        ],
        cost_estimate=pl.CostEstimate(
            flops=4 * nq * nk * width, transcendentals=nq * nk, bytes_accessed=2 * (2 * nq * width + 2 * nk * width)
        ),
        compiler_params=pltpu.CompilerParams(
            collective_id=collective_id, has_side_effects=True, vmem_limit_bytes=48 * 1024 * 1024
        ),
    )(length.reshape(1), queries, keys_in, values_in)


def shards(enc_query, enc_key, enc_value, sum_query, doc_len, w_memory):
    length = doc_len[0]
    n_seq = lax.axis_size("seq")
    core = lax.axis_index("seq") % 2
    sibling = [(i, i ^ 1) for i in range(n_seq)]
    half = w_memory.shape[2] // 2
    w_half = lax.dynamic_slice_in_dim(w_memory, core * half, half, axis=2)
    w_pair = lax.ppermute(w_half, "doc_x", perm=[(0, 1), (1, 0)])
    w_half = jnp.where(lax.axis_index("doc_x") == 0, jnp.concatenate([w_half, w_pair], axis=2),
                       jnp.concatenate([w_pair, w_half], axis=2))
    w_half = lax.all_gather(w_half, "doc_y", axis=2, tiled=True)

    rows, sum_rows = enc_query.shape[1], sum_query.shape[1]
    mixed = lax.all_to_all(
        jnp.concatenate([enc_query[0], enc_key[0], enc_value[0], sum_query[0]], axis=0),
        "seq", split_axis=1, concat_axis=0, tiled=True,
    ).reshape(n_seq, 3 * rows + sum_rows, -1)
    head_query, head_key, head_value = (mixed[:, i * rows:(i + 1) * rows].reshape(n_seq * rows, -1) for i in range(3))
    summary_heads = mixed[:, 3 * rows:].reshape(n_seq * sum_rows, -1)
    by_head = attend_scatter(head_query, head_key, head_value, length, n_seq, 1)
    encoder_out = by_head.transpose(1, 0, 2).reshape(by_head.shape[1], -1)

    enc_pair = jnp.concatenate([encoder_out, lax.ppermute(encoder_out, "seq", sibling)], axis=0)
    made = jnp.einsum("tf,kfc->ktc", enc_pair, w_half, preferred_element_type=jnp.float32).astype(jnp.bfloat16)
    made = made.reshape(2, 2, rows, -1, half).transpose(1, 3, 0, 2, 4)
    own, received = made[0], lax.ppermute(made[1], "seq", sibling)
    by_head = jnp.where(core == 0, jnp.stack([own, received], axis=1), jnp.stack([received, own], axis=1))
    by_head = by_head.reshape(n_seq, 2, rows, half)
    memory = lax.all_to_all(by_head, "seq", split_axis=0, concat_axis=2, tiled=True)
    memory_keys, memory_values = memory[0, 0], memory[0, 1]
    answer = attend_scatter(summary_heads, memory_keys, memory_values, length, n_seq, 2)
    summary_out = answer.transpose(1, 0, 2).reshape(answer.shape[1], -1)
    return (encoder_out[None], summary_out[None])


def solution(mesh):
    n_doc = mesh.shape["doc"]
    split = jax.sharding.Mesh(mesh.devices.reshape(n_doc // 2, 2, mesh.shape["seq"]), ("doc_y", "doc_x", "seq"))
    doc = ("doc_y", "doc_x")
    in_specs = (
        P(doc, "seq", None),
        P(doc, "seq", None),
        P(doc, "seq", None),
        P(doc, "seq", None),
        P(doc),
        P(None, None, doc),
    )
    out_specs = (P(doc, "seq", None), P(doc, "seq", None))
    return jax.shard_map(shards, mesh=split, in_specs=in_specs, out_specs=out_specs, check_vma=False)
```

```python
import jax
import jax.numpy as jnp
from jax import lax
from jax.experimental import pallas as pl
from jax.experimental.pallas import tpu as pltpu
from jax.sharding import PartitionSpec as P

HEAD_DIM = 64


def _attend_kernel(len_ref, q_ref, k_ref, v_ref, o_ref):
    scores = lax.dot_general(
        q_ref[...], k_ref[...], (((1,), (1,)), ((), ())), preferred_element_type=jnp.float32
    ) * HEAD_DIM ** (-0.5)
    key_pos = lax.broadcasted_iota(jnp.int32, scores.shape, 1)
    scores = jnp.where(key_pos < len_ref[0], scores, -1e30)
    row_max = jnp.max(scores, axis=1, keepdims=True)
    weights = jnp.exp(scores - row_max)
    denominator = jnp.sum(weights, axis=1, keepdims=True)
    weighted = jnp.dot(weights.astype(jnp.bfloat16), v_ref[...], preferred_element_type=jnp.float32)
    o_ref[...] = (weighted / denominator).astype(o_ref.dtype)


def attend_head(queries, keys_in, values_in, length, block_rows=256):
    nq, width = queries.shape
    nk = keys_in.shape[0]
    block_rows = min(block_rows, nq)
    grid_spec = pltpu.PrefetchScalarGridSpec(
        num_scalar_prefetch=1,
        grid=(nq // block_rows,),
        in_specs=[
            pl.BlockSpec((block_rows, width), lambda i, n: (i, 0)),
            pl.BlockSpec((nk, width), lambda i, n: (0, 0)),
            pl.BlockSpec((nk, width), lambda i, n: (0, 0)),
        ],
        out_specs=pl.BlockSpec((block_rows, width), lambda i, n: (i, 0)),
    )
    cost = pl.CostEstimate(
        flops=4 * nq * nk * width,
        transcendentals=nq * nk,
        bytes_accessed=2 * (2 * nq * width + 2 * nk * width),
    )
    return pl.pallas_call(
        _attend_kernel,
        grid_spec=grid_spec,
        out_shape=jax.ShapeDtypeStruct((nq, width), jnp.bfloat16),
        cost_estimate=cost,
        compiler_params=pltpu.CompilerParams(vmem_limit_bytes=48 * 1024 * 1024),
    )(length.reshape(1), queries, keys_in, values_in)


MESH = pl.DeviceIdType.MESH


def _attend_scatter_kernel(len_ref, x_ref, out_ref, ctx_buf, send_sem, recv_sem, own_sem):
    n_dev, chunk = out_ref.shape[0], out_ref.shape[1]
    me = lax.axis_index("seq")
    place = (lax.axis_index("doc_y"), lax.axis_index("doc_x"))
    barrier = pltpu.get_barrier_semaphore()

    def greet(t, carry):
        @pl.when(t != me)
        def _():
            pl.semaphore_signal(barrier, inc=1, device_id=place + (t,), device_id_type=MESH)

        return carry

    lax.fori_loop(0, n_dev, greet, 0)
    pl.semaphore_wait(barrier, n_dev - 1)
    length = len_ref[0]

    def block(step, carry):
        b = lax.rem(step + me // 2, n_dev // 2)
        queries = x_ref[pl.ds(2 * b, 2), 0:chunk, :].reshape(2 * chunk, -1)
        keys = x_ref[:, chunk:2 * chunk, :].reshape(n_dev * chunk, -1)
        scores = lax.dot_general(
            queries, keys, (((1,), (1,)), ((), ())), preferred_element_type=jnp.float32
        ) * HEAD_DIM ** (-0.5)
        key_pos = lax.broadcasted_iota(jnp.int32, scores.shape, 1)
        scores = jnp.where(key_pos < length, scores, -1e30)
        row_max = jnp.max(scores, axis=1, keepdims=True)
        weights = jnp.exp(scores - row_max)
        denominator = jnp.sum(weights, axis=1, keepdims=True)
        values = x_ref[:, 2 * chunk:3 * chunk, :].reshape(n_dev * chunk, -1)
        weighted = jnp.dot(weights.astype(jnp.bfloat16), values, preferred_element_type=jnp.float32)
        context = (weighted / denominator).astype(jnp.bfloat16)
        ctx_buf[pl.ds(2 * b, 2)] = context.reshape(2, chunk, context.shape[1])
        for j in range(2):
            owner = 2 * b + j

            @pl.when(owner != me)
            def _():
                pltpu.make_async_remote_copy(
                    src_ref=ctx_buf.at[owner], dst_ref=out_ref.at[me], send_sem=send_sem, recv_sem=recv_sem,
                    device_id=place + (owner,), device_id_type=MESH,
                ).start()

        return carry

    lax.fori_loop(0, n_dev // 2, block, 0)
    own = pltpu.make_async_copy(ctx_buf.at[me], out_ref.at[me], own_sem)
    own.start()
    every = pltpu.make_async_remote_copy(
        src_ref=ctx_buf.at[pl.ds(0, n_dev - 1)], dst_ref=out_ref.at[pl.ds(0, n_dev - 1)], send_sem=send_sem,
        recv_sem=recv_sem, device_id=place + (me,), device_id_type=MESH,
    )
    every.wait_send()
    every.wait_recv()
    own.wait()


def attend_scatter(mixed, length, n_dev, chunk):
    width = mixed.shape[2]
    nq = nk = n_dev * chunk
    vmem = pl.BlockSpec(memory_space=pltpu.VMEM)
    return pl.pallas_call(
        _attend_scatter_kernel,
        out_shape=jax.ShapeDtypeStruct((n_dev, chunk, width), jnp.bfloat16),
        in_specs=[pl.BlockSpec(memory_space=pltpu.SMEM), vmem],
        out_specs=pl.BlockSpec(memory_space=pl.ANY),
        scratch_shapes=[
            pltpu.VMEM((n_dev, chunk, width), jnp.bfloat16),
            pltpu.SemaphoreType.DMA,
            pltpu.SemaphoreType.DMA,
            pltpu.SemaphoreType.DMA,
        ],
        cost_estimate=pl.CostEstimate(
            flops=4 * nq * nk * width, transcendentals=nq * nk, bytes_accessed=2 * (2 * nq * width + 2 * nk * width)
        ),
        compiler_params=pltpu.CompilerParams(
            collective_id=1, has_side_effects=True, vmem_limit_bytes=48 * 1024 * 1024
        ),
    )(length.reshape(1), mixed)


def shards(enc_query, enc_key, enc_value, sum_query, doc_len, w_memory):
    length = doc_len[0]
    n_seq = lax.axis_size("seq")
    core = lax.axis_index("seq") % 2
    sibling = [(i, i ^ 1) for i in range(n_seq)]
    half = w_memory.shape[2] // 2
    w_half = lax.dynamic_slice_in_dim(w_memory, core * half, half, axis=2)
    w_pair = lax.ppermute(w_half, "doc_x", perm=[(0, 1), (1, 0)])
    w_half = jnp.where(lax.axis_index("doc_x") == 0, jnp.concatenate([w_half, w_pair], axis=2),
                       jnp.concatenate([w_pair, w_half], axis=2))
    w_half = lax.all_gather(w_half, "doc_y", axis=2, tiled=True)

    rows, sum_rows = enc_query.shape[1], sum_query.shape[1]
    mixed = jnp.concatenate([enc_query[0], enc_key[0], enc_value[0], sum_query[0]], axis=0)
    mixed = mixed.reshape(3 * rows + sum_rows, n_seq, -1).transpose(1, 0, 2)
    mixed = lax.all_to_all(mixed, "seq", split_axis=0, concat_axis=0, tiled=True)
    summary_heads = mixed[:, 3 * rows:].reshape(n_seq * sum_rows, -1)
    by_head = attend_scatter(mixed, length, n_seq, rows)
    encoder_out = by_head.transpose(1, 0, 2).reshape(by_head.shape[1], -1)

    enc_pair = jnp.concatenate([encoder_out, lax.ppermute(encoder_out, "seq", sibling)], axis=0)
    made = jnp.einsum("tf,kfc->ktc", enc_pair, w_half, preferred_element_type=jnp.float32).astype(jnp.bfloat16)
    made = made.reshape(2, 2, rows, -1, half).transpose(1, 3, 0, 2, 4)
    own, received = made[0], lax.ppermute(made[1], "seq", sibling)
    by_head = jnp.where(core == 0, jnp.stack([own, received], axis=1), jnp.stack([received, own], axis=1))
    by_head = by_head.reshape(n_seq, 2, rows, half)
    memory = lax.all_to_all(by_head, "seq", split_axis=0, concat_axis=2, tiled=True)
    memory_keys, memory_values = memory[0, 0], memory[0, 1]
    answer = attend_head(summary_heads, memory_keys, memory_values, length)
    summary_out = lax.all_to_all(answer, "seq", split_axis=0, concat_axis=1, tiled=True)
    return (encoder_out[None], summary_out[None])


def solution(mesh):
    n_doc = mesh.shape["doc"]
    split = jax.sharding.Mesh(mesh.devices.reshape(n_doc // 2, 2, mesh.shape["seq"]), ("doc_y", "doc_x", "seq"))
    doc = ("doc_y", "doc_x")
    in_specs = (
        P(doc, "seq", None),
        P(doc, "seq", None),
        P(doc, "seq", None),
        P(doc, "seq", None),
        P(doc),
        P(None, None, doc),
    )
    out_specs = (P(doc, "seq", None), P(doc, "seq", None))
    return jax.shard_map(shards, mesh=split, in_specs=in_specs, out_specs=out_specs, check_vma=False)
```

```python
import jax
import jax.numpy as jnp
from jax import lax
from jax.experimental import pallas as pl
from jax.experimental.pallas import tpu as pltpu
from jax.sharding import PartitionSpec as P

HEAD_DIM = 64


def _attend_kernel(len_ref, q_ref, k_ref, v_ref, o_ref):
    scores = lax.dot_general(
        q_ref[...], k_ref[...], (((1,), (1,)), ((), ())), preferred_element_type=jnp.float32
    ) * HEAD_DIM ** (-0.5)
    key_pos = lax.broadcasted_iota(jnp.int32, scores.shape, 1)
    scores = jnp.where(key_pos < len_ref[0], scores, -1e30)
    row_max = jnp.max(scores, axis=1, keepdims=True)
    weights = jnp.exp(scores - row_max)
    denominator = jnp.sum(weights, axis=1, keepdims=True)
    weighted = jnp.dot(weights.astype(jnp.bfloat16), v_ref[...], preferred_element_type=jnp.float32)
    o_ref[...] = (weighted / denominator).astype(o_ref.dtype)


def attend_head(queries, keys_in, values_in, length, block_rows=256):
    nq, width = queries.shape
    nk = keys_in.shape[0]
    block_rows = min(block_rows, nq)
    grid_spec = pltpu.PrefetchScalarGridSpec(
        num_scalar_prefetch=1,
        grid=(nq // block_rows,),
        in_specs=[
            pl.BlockSpec((block_rows, width), lambda i, n: (i, 0)),
            pl.BlockSpec((nk, width), lambda i, n: (0, 0)),
            pl.BlockSpec((nk, width), lambda i, n: (0, 0)),
        ],
        out_specs=pl.BlockSpec((block_rows, width), lambda i, n: (i, 0)),
    )
    cost = pl.CostEstimate(
        flops=4 * nq * nk * width,
        transcendentals=nq * nk,
        bytes_accessed=2 * (2 * nq * width + 2 * nk * width),
    )
    return pl.pallas_call(
        _attend_kernel,
        grid_spec=grid_spec,
        out_shape=jax.ShapeDtypeStruct((nq, width), jnp.bfloat16),
        cost_estimate=cost,
        compiler_params=pltpu.CompilerParams(vmem_limit_bytes=48 * 1024 * 1024),
    )(length.reshape(1), queries, keys_in, values_in)


MESH = pl.DeviceIdType.MESH


def _attend_scatter_kernel(len_ref, x_ref, out_ref, ctx_buf, send_sem, recv_sem, own_sem):
    n_dev, chunk = out_ref.shape[0], out_ref.shape[1]
    me = lax.axis_index("seq")
    place = (lax.axis_index("doc_y"), lax.axis_index("doc_x"))
    barrier = pltpu.get_barrier_semaphore()

    def greet(t, carry):
        @pl.when(t != me)
        def _():
            pl.semaphore_signal(barrier, inc=1, device_id=place + (t,), device_id_type=MESH)

        return carry

    lax.fori_loop(0, n_dev, greet, 0)
    pl.semaphore_wait(barrier, n_dev - 1)
    length = len_ref[0]

    def block(step, carry):
        b = lax.rem(step + me // 2 + 1, n_dev // 2)
        queries = x_ref[pl.ds(2 * b, 2), 0:chunk, :].reshape(2 * chunk, -1)
        keys = x_ref[:, chunk:2 * chunk, :].reshape(n_dev * chunk, -1)
        scores = lax.dot_general(
            queries, keys, (((1,), (1,)), ((), ())), preferred_element_type=jnp.float32
        ) * HEAD_DIM ** (-0.5)
        key_pos = lax.broadcasted_iota(jnp.int32, scores.shape, 1)
        scores = jnp.where(key_pos < length, scores, -1e30)
        row_max = jnp.max(scores, axis=1, keepdims=True)
        weights = jnp.exp(scores - row_max)
        denominator = jnp.sum(weights, axis=1, keepdims=True)
        values = x_ref[:, 2 * chunk:3 * chunk, :].reshape(n_dev * chunk, -1)
        weighted = jnp.dot(weights.astype(jnp.bfloat16), values, preferred_element_type=jnp.float32)
        context = (weighted / denominator).astype(jnp.bfloat16)
        ctx_buf[pl.ds(2 * b, 2)] = context.reshape(2, chunk, context.shape[1])
        for j in range(2):
            owner = 2 * b + j

            @pl.when(owner != me)
            def _():
                pltpu.make_async_remote_copy(
                    src_ref=ctx_buf.at[owner], dst_ref=out_ref.at[me], send_sem=send_sem, recv_sem=recv_sem,
                    device_id=place + (owner,), device_id_type=MESH,
                ).start()

        return carry

    lax.fori_loop(0, n_dev // 2, block, 0)
    own = pltpu.make_async_copy(ctx_buf.at[me], out_ref.at[me], own_sem)
    own.start()
    every = pltpu.make_async_remote_copy(
        src_ref=ctx_buf.at[pl.ds(0, n_dev - 1)], dst_ref=out_ref.at[pl.ds(0, n_dev - 1)], send_sem=send_sem,
        recv_sem=recv_sem, device_id=place + (me,), device_id_type=MESH,
    )
    every.wait_send()
    every.wait_recv()
    own.wait()


def attend_scatter(mixed, length, n_dev, chunk):
    width = mixed.shape[2]
    nq = nk = n_dev * chunk
    vmem = pl.BlockSpec(memory_space=pltpu.VMEM)
    return pl.pallas_call(
        _attend_scatter_kernel,
        out_shape=jax.ShapeDtypeStruct((n_dev, chunk, width), jnp.bfloat16),
        in_specs=[pl.BlockSpec(memory_space=pltpu.SMEM), vmem],
        out_specs=pl.BlockSpec(memory_space=pl.ANY),
        scratch_shapes=[
            pltpu.VMEM((n_dev, chunk, width), jnp.bfloat16),
            pltpu.SemaphoreType.DMA,
            pltpu.SemaphoreType.DMA,
            pltpu.SemaphoreType.DMA,
        ],
        cost_estimate=pl.CostEstimate(
            flops=4 * nq * nk * width, transcendentals=nq * nk, bytes_accessed=2 * (2 * nq * width + 2 * nk * width)
        ),
        compiler_params=pltpu.CompilerParams(
            collective_id=1, has_side_effects=True, vmem_limit_bytes=48 * 1024 * 1024
        ),
    )(length.reshape(1), mixed)


def shards(enc_query, enc_key, enc_value, sum_query, doc_len, w_memory):
    length = doc_len[0]
    n_seq = lax.axis_size("seq")
    core = lax.axis_index("seq") % 2
    sibling = [(i, i ^ 1) for i in range(n_seq)]
    half = w_memory.shape[2] // 2
    w_half = lax.dynamic_slice_in_dim(w_memory, core * half, half, axis=2)
    w_pair = lax.ppermute(w_half, "doc_x", perm=[(0, 1), (1, 0)])
    w_half = jnp.where(lax.axis_index("doc_x") == 0, jnp.concatenate([w_half, w_pair], axis=2),
                       jnp.concatenate([w_pair, w_half], axis=2))
    w_half = lax.all_gather(w_half, "doc_y", axis=2, tiled=True)

    rows, sum_rows = enc_query.shape[1], sum_query.shape[1]
    mixed = jnp.concatenate([enc_query[0], enc_key[0], enc_value[0], sum_query[0]], axis=0)
    mixed = mixed.reshape(3 * rows + sum_rows, n_seq, -1).transpose(1, 0, 2)
    mixed = lax.all_to_all(mixed, "seq", split_axis=0, concat_axis=0, tiled=True)
    summary_heads = mixed[:, 3 * rows:].reshape(n_seq * sum_rows, -1)
    by_head = attend_scatter(mixed, length, n_seq, rows)
    encoder_out = by_head.transpose(1, 0, 2).reshape(by_head.shape[1], -1)

    enc_pair = jnp.concatenate([encoder_out, lax.ppermute(encoder_out, "seq", sibling)], axis=0)
    made = jnp.einsum("tf,kfc->ktc", enc_pair, w_half, preferred_element_type=jnp.float32).astype(jnp.bfloat16)
    made = made.reshape(2, 2, rows, -1, half).transpose(1, 3, 0, 2, 4)
    own, received = made[0], lax.ppermute(made[1], "seq", sibling)
    by_head = jnp.where(core == 0, jnp.stack([own, received], axis=1), jnp.stack([received, own], axis=1))
    by_head = by_head.reshape(n_seq, 2, rows, half)
    memory = lax.all_to_all(by_head, "seq", split_axis=0, concat_axis=2, tiled=True)
    memory_keys, memory_values = memory[0, 0], memory[0, 1]
    answer = attend_head(summary_heads, memory_keys, memory_values, length)
    summary_out = lax.all_to_all(answer, "seq", split_axis=0, concat_axis=1, tiled=True)
    return (encoder_out[None], summary_out[None])


def solution(mesh):
    n_doc = mesh.shape["doc"]
    split = jax.sharding.Mesh(mesh.devices.reshape(n_doc // 2, 2, mesh.shape["seq"]), ("doc_y", "doc_x", "seq"))
    doc = ("doc_y", "doc_x")
    in_specs = (
        P(doc, "seq", None),
        P(doc, "seq", None),
        P(doc, "seq", None),
        P(doc, "seq", None),
        P(doc),
        P(None, None, doc),
    )
    out_specs = (P(doc, "seq", None), P(doc, "seq", None))
    return jax.shard_map(shards, mesh=split, in_specs=in_specs, out_specs=out_specs, check_vma=False)
```

```python
import jax
import jax.numpy as jnp
from jax import lax
from jax.experimental import pallas as pl
from jax.experimental.pallas import tpu as pltpu
from jax.sharding import PartitionSpec as P

HEAD_DIM = 64


def _attend_kernel(len_ref, q_ref, k_ref, v_ref, o_ref):
    scores = lax.dot_general(
        q_ref[...], k_ref[...], (((1,), (1,)), ((), ())), preferred_element_type=jnp.float32
    ) * HEAD_DIM ** (-0.5)
    key_pos = lax.broadcasted_iota(jnp.int32, scores.shape, 1)
    scores = jnp.where(key_pos < len_ref[0], scores, -1e30)
    row_max = jnp.max(scores, axis=1, keepdims=True)
    weights = jnp.exp(scores - row_max)
    denominator = jnp.sum(weights, axis=1, keepdims=True)
    weighted = jnp.dot(weights.astype(jnp.bfloat16), v_ref[...], preferred_element_type=jnp.float32)
    o_ref[...] = (weighted / denominator).astype(o_ref.dtype)


def attend_head(queries, keys_in, values_in, length, block_rows=256):
    nq, width = queries.shape
    nk = keys_in.shape[0]
    block_rows = min(block_rows, nq)
    grid_spec = pltpu.PrefetchScalarGridSpec(
        num_scalar_prefetch=1,
        grid=(nq // block_rows,),
        in_specs=[
            pl.BlockSpec((block_rows, width), lambda i, n: (i, 0)),
            pl.BlockSpec((nk, width), lambda i, n: (0, 0)),
            pl.BlockSpec((nk, width), lambda i, n: (0, 0)),
        ],
        out_specs=pl.BlockSpec((block_rows, width), lambda i, n: (i, 0)),
    )
    cost = pl.CostEstimate(
        flops=4 * nq * nk * width,
        transcendentals=nq * nk,
        bytes_accessed=2 * (2 * nq * width + 2 * nk * width),
    )
    return pl.pallas_call(
        _attend_kernel,
        grid_spec=grid_spec,
        out_shape=jax.ShapeDtypeStruct((nq, width), jnp.bfloat16),
        cost_estimate=cost,
        compiler_params=pltpu.CompilerParams(vmem_limit_bytes=48 * 1024 * 1024),
    )(length.reshape(1), queries, keys_in, values_in)


MESH = pl.DeviceIdType.MESH


def _attend_scatter_kernel(len_ref, x_ref, out_ref, ctx_buf, send_sem, recv_sem, own_sem):
    n_dev, chunk = out_ref.shape[0], out_ref.shape[1]
    group = 4
    me = lax.axis_index("seq")
    place = (lax.axis_index("doc_y"), lax.axis_index("doc_x"))
    barrier = pltpu.get_barrier_semaphore()

    def greet(t, carry):
        @pl.when(t != me)
        def _():
            pl.semaphore_signal(barrier, inc=1, device_id=place + (t,), device_id_type=MESH)

        return carry

    lax.fori_loop(0, n_dev, greet, 0)
    pl.semaphore_wait(barrier, n_dev - 1)
    length = len_ref[0]

    def block(step, carry):
        b = lax.rem(step + me // group + 1, n_dev // group)
        queries = x_ref[pl.ds(group * b, group), 0:chunk, :].reshape(group * chunk, -1)
        keys = x_ref[:, chunk:2 * chunk, :].reshape(n_dev * chunk, -1)
        scores = lax.dot_general(
            queries, keys, (((1,), (1,)), ((), ())), preferred_element_type=jnp.float32
        ) * HEAD_DIM ** (-0.5)
        key_pos = lax.broadcasted_iota(jnp.int32, scores.shape, 1)
        scores = jnp.where(key_pos < length, scores, -1e30)
        row_max = jnp.max(scores, axis=1, keepdims=True)
        weights = jnp.exp(scores - row_max)
        denominator = jnp.sum(weights, axis=1, keepdims=True)
        values = x_ref[:, 2 * chunk:3 * chunk, :].reshape(n_dev * chunk, -1)
        weighted = jnp.dot(weights.astype(jnp.bfloat16), values, preferred_element_type=jnp.float32)
        context = (weighted / denominator).astype(jnp.bfloat16)
        ctx_buf[pl.ds(group * b, group)] = context.reshape(group, chunk, context.shape[1])
        for j in range(group):
            owner = group * b + j

            @pl.when(owner != me)
            def _():
                pltpu.make_async_remote_copy(
                    src_ref=ctx_buf.at[owner], dst_ref=out_ref.at[me], send_sem=send_sem, recv_sem=recv_sem,
                    device_id=place + (owner,), device_id_type=MESH,
                ).start()

        return carry

    lax.fori_loop(0, n_dev // group, block, 0)
    own = pltpu.make_async_copy(ctx_buf.at[me], out_ref.at[me], own_sem)
    own.start()
    every = pltpu.make_async_remote_copy(
        src_ref=ctx_buf.at[pl.ds(0, n_dev - 1)], dst_ref=out_ref.at[pl.ds(0, n_dev - 1)], send_sem=send_sem,
        recv_sem=recv_sem, device_id=place + (me,), device_id_type=MESH,
    )
    every.wait_send()
    every.wait_recv()
    own.wait()


def attend_scatter(mixed, length, n_dev, chunk):
    width = mixed.shape[2]
    nq = nk = n_dev * chunk
    vmem = pl.BlockSpec(memory_space=pltpu.VMEM)
    return pl.pallas_call(
        _attend_scatter_kernel,
        out_shape=jax.ShapeDtypeStruct((n_dev, chunk, width), jnp.bfloat16),
        in_specs=[pl.BlockSpec(memory_space=pltpu.SMEM), vmem],
        out_specs=pl.BlockSpec(memory_space=pl.ANY),
        scratch_shapes=[
            pltpu.VMEM((n_dev, chunk, width), jnp.bfloat16),
            pltpu.SemaphoreType.DMA,
            pltpu.SemaphoreType.DMA,
            pltpu.SemaphoreType.DMA,
        ],
        cost_estimate=pl.CostEstimate(
            flops=4 * nq * nk * width, transcendentals=nq * nk, bytes_accessed=2 * (2 * nq * width + 2 * nk * width)
        ),
        compiler_params=pltpu.CompilerParams(
            collective_id=1, has_side_effects=True, vmem_limit_bytes=48 * 1024 * 1024
        ),
    )(length.reshape(1), mixed)


def shards(enc_query, enc_key, enc_value, sum_query, doc_len, w_memory):
    length = doc_len[0]
    n_seq = lax.axis_size("seq")
    core = lax.axis_index("seq") % 2
    sibling = [(i, i ^ 1) for i in range(n_seq)]
    half = w_memory.shape[2] // 2
    w_half = lax.dynamic_slice_in_dim(w_memory, core * half, half, axis=2)
    w_pair = lax.ppermute(w_half, "doc_x", perm=[(0, 1), (1, 0)])
    w_half = jnp.where(lax.axis_index("doc_x") == 0, jnp.concatenate([w_half, w_pair], axis=2),
                       jnp.concatenate([w_pair, w_half], axis=2))
    w_half = lax.all_gather(w_half, "doc_y", axis=2, tiled=True)

    rows, sum_rows = enc_query.shape[1], sum_query.shape[1]
    mixed = jnp.concatenate([enc_query[0], enc_key[0], enc_value[0], sum_query[0]], axis=0)
    mixed = mixed.reshape(3 * rows + sum_rows, n_seq, -1).transpose(1, 0, 2)
    mixed = lax.all_to_all(mixed, "seq", split_axis=0, concat_axis=0, tiled=True)
    summary_heads = mixed[:, 3 * rows:].reshape(n_seq * sum_rows, -1)
    by_head = attend_scatter(mixed, length, n_seq, rows)
    encoder_out = by_head.transpose(1, 0, 2).reshape(by_head.shape[1], -1)

    enc_pair = jnp.concatenate([encoder_out, lax.ppermute(encoder_out, "seq", sibling)], axis=0)
    made = jnp.einsum("tf,kfc->ktc", enc_pair, w_half, preferred_element_type=jnp.float32).astype(jnp.bfloat16)
    made = made.reshape(2, 2, rows, -1, half).transpose(1, 3, 0, 2, 4)
    own, received = made[0], lax.ppermute(made[1], "seq", sibling)
    by_head = jnp.where(core == 0, jnp.stack([own, received], axis=1), jnp.stack([received, own], axis=1))
    by_head = by_head.reshape(n_seq, 2, rows, half)
    memory = lax.all_to_all(by_head, "seq", split_axis=0, concat_axis=2, tiled=True)
    memory_keys, memory_values = memory[0, 0], memory[0, 1]
    answer = attend_head(summary_heads, memory_keys, memory_values, length)
    summary_out = lax.all_to_all(answer, "seq", split_axis=0, concat_axis=1, tiled=True)
    return (encoder_out[None], summary_out[None])


def solution(mesh):
    n_doc = mesh.shape["doc"]
    split = jax.sharding.Mesh(mesh.devices.reshape(n_doc // 2, 2, mesh.shape["seq"]), ("doc_y", "doc_x", "seq"))
    doc = ("doc_y", "doc_x")
    in_specs = (
        P(doc, "seq", None),
        P(doc, "seq", None),
        P(doc, "seq", None),
        P(doc, "seq", None),
        P(doc),
        P(None, None, doc),
    )
    out_specs = (P(doc, "seq", None), P(doc, "seq", None))
    return jax.shard_map(shards, mesh=split, in_specs=in_specs, out_specs=out_specs, check_vma=False)
```
